32 devices in a mesh: seq: 8 (over z, y), tp: 4 (over x, core).
Axes of the slice: x: 2, y: 2, z: 4, core: 2. Of those that a mesh axis runs over, the one named last changes fastest.
Arguments:
- tokens: bfloat16 [6144, 2048], P('seq'), may hold values from -7 to 7
- seg_ids: int32 [6144], P('seq'), may hold values from 0 to 3, never falling along the last dimension, each value on 1 to 3072 neighbouring positions
- norm1_gain: bfloat16 [2048], replicated, may hold values from 0.25 to 1.75
- w_mix: bfloat16 [2048, 16, 768], P(None, 'tp'), may hold values from -0.125 to 0.125
- w_rate: bfloat16 [2048, 16, 2], P(None, 'tp'), may hold values from -1 to 1
- conv_w: bfloat16 [4, 16, 512], P(None, 'tp'), may hold values from -3 to 3
- a_log: float32 [16], P('tp'), may hold values from -12 to -2.8
- dt_bias: float32 [16], P('tp'), may hold values from -1 to 1
- out_gain: bfloat16 [256], replicated, may hold values from 0.25 to 1.75
- w_out: bfloat16 [2048, 16, 256], P(None, 'tp'), may hold values from -0.1875 to 0.1875
- norm2_gain: bfloat16 [2048], replicated, may hold values from 0.25 to 1.75
- w_up: bfloat16 [2048, 2, 5632], P(None, None, 'tp'), may hold values from -0.125 to 0.125
- w_down: bfloat16 [2048, 5632], P(None, 'tp'), may hold values from -0.15625 to 0.15625
- cotangent: bfloat16 [6144, 2048], P('seq'), may hold values from -6 to 6
Outputs:
- layer_out: bfloat16 [6144, 2048], P('seq')
- grad_tokens: bfloat16 [6144, 2048], P('seq')
- grad_norm1: float32 [2048], replicated
- grad_mix: float32 [2048, 16, 768], P('seq', 'tp')
- grad_rate: float32 [2048, 16, 2], P('seq', 'tp')
- grad_conv: float32 [4, 16, 512], replicated
- grad_a_log: float32 [16], replicated
- grad_dt_bias: float32 [16], replicated
- grad_out_gain: float32 [256], replicated
- grad_w_out: float32 [2048, 16, 256], P('seq', 'tp')
- grad_norm2: float32 [2048], replicated
- grad_up: float32 [2048, 2, 5632], P('seq', None, 'tp')
- grad_down: float32 [2048, 5632], P('seq', 'tp')
The draws below stay inside these ranges and needn't reach their ends.
Inputs may be any that keep to these rules, and one draw needn't show every extreme that they name: `seg_ids`: document ids of the packed stream, never falling: each of the 4 documents is one contiguous run of tokens, the longest exactly 3072 tokens.
All inputs are finite; a program needn't handle non-finite values.
Results may differ from the reference program's by a relative error of at most 0.02.
Values may be sent and summed in bfloat16 or wider, within the bound.
A program may use at most 384 MiB of HBM per device.

```python
import math
import jax
import jax.numpy as jnp
import numpy as np
from jax import lax

D = 2048
H = 16
DK = 128
DV = 256
FF = 5632
TAPS = 4
GROUP = 64
DOCS = 4
TOKENS = 6144
SEG_MOST = 3072


def shared_mean(key):
    return jnp.clip(jax.random.normal(jax.random.fold_in(key, 7001), (D,), jnp.float32), -3.0, 3.0)


def draw_tokens(key, part):
    common = 0.6 * shared_mean(key)
    noise_key = jax.random.fold_in(key, 7002)
    noise_rows = jnp.clip(jax.random.normal(noise_key, (TOKENS, D), jnp.float32), -5.0, 5.0)
    return (noise_rows + common[None, :]).astype(jnp.bfloat16)


def draw_w_rate(key, part):
    common = shared_mean(key)
    first_key = jax.random.fold_in(key, 7003)
    second_key = jax.random.fold_in(key, 7004)
    decay_cols = jnp.clip(jax.random.normal(first_key, (D, H), jnp.float32), -6.0, 6.0) * D ** (-0.5)
    spread_cols = jnp.clip(jax.random.normal(second_key, (D, H), jnp.float32), -4.0, 4.0) * (0.6 * D ** (-0.5))
    write_cols = spread_cols - 7.8 / D * common[:, None]
    return jnp.stack([decay_cols, write_cols], axis=-1).astype(jnp.bfloat16)


def draw_a_log(key, part):
    slow_rates = jax.random.uniform(jax.random.fold_in(key, 7005), (H,), jnp.float32, -12.0, -9.5)
    fast_rates = jax.random.uniform(jax.random.fold_in(key, 7006), (H,), jnp.float32, -4.0, -2.8)
    picked = jax.random.permutation(jax.random.fold_in(key, 7008), H) < H // 2
    return jnp.where(picked, fast_rates, slow_rates)


def levels(rng, dims, pieces, smallest, high):
    level = 1.0
    for position, parts in pieces:
        steps = jax.random.uniform(jax.random.fold_in(jax.random.fold_in(rng, 6), position), (parts,), jnp.float32, smallest / len(pieces), high / len(pieces))
        level = level * jnp.repeat(jnp.exp(steps), dims[position] // parts).reshape((-1,) + (1,) * (len(dims) - 1 - position))
    return level


def profile(count, total, most, skew):
    weights = [(1 << 20) // math.isqrt(rank ** skew) + 1 for rank in range(2, count + 1)]
    surplus, holding = total - most - (count - 1), [1] * (count - 1)
    while surplus > 0:
        free = [i for i in range(count - 1) if holding[i] < most]
        whole, budget = sum([weights[i] for i in free]), surplus
        for i in free:
            extra = min(most - holding[i], max(1, budget * weights[i] // whole), surplus)
            holding[i] = holding[i] + extra
            surplus = surplus - extra
    return np.array([most] + holding)


def ragged(own_key, number_of, total, reach, lean):
    if number_of == 2:
        one = jax.random.randint(own_key, (), max(1, total - reach), min(reach, total - 1) + 1)
        return jnp.stack([one, total - one])
    sizes = jnp.asarray(profile(number_of, total, reach, lean), jnp.int32)
    pairs = (number_of - 1) // 2
    giver, sink = sizes[1:1 + 2 * pairs:2], sizes[2:2 + 2 * pairs:2]
    margin = jnp.minimum(giver - 1, reach - sink)
    passed = jax.random.randint(jax.random.fold_in(own_key, 1), (pairs,), 0, 1 << 20) % (margin + 1)
    sizes = sizes.at[1:1 + 2 * pairs:2].set(giver - passed).at[2:2 + 2 * pairs:2].set(sink + passed)
    return sizes[jax.random.permutation(jax.random.fold_in(own_key, 2), number_of)]


def gaussian(rng, shape, spread, bound, shards=(), held_as=jnp.bfloat16):
    entries = spread * jax.random.normal(rng, shape, jnp.float32)
    if shards:
        entries = entries * levels(rng, shape, shards, -0.22, 0.18)
    return jnp.clip(entries, -bound, bound).astype(held_as)


def setup_inputs(seed: int = 0) -> dict:
    arg_keys = jax.random.split(jax.random.key(seed), 15)
    return {
        "tokens": draw_tokens(jax.random.fold_in(arg_keys[14], 71), 0),
        "seg_ids": jnp.searchsorted(jnp.cumsum(ragged(arg_keys[1], DOCS, TOKENS, SEG_MOST, 2)), jnp.arange(TOKENS), side="right").astype(jnp.int32),
        "norm1_gain": jnp.clip(1.0 + 0.15 * jax.random.normal(arg_keys[2], (D,), jnp.float32), 0.25, 1.75).astype(jnp.bfloat16),
        "w_mix": gaussian(arg_keys[3], (D, H, 2 * DK + 2 * DV), D ** -0.5, 0.125, ((1, 4),)),
        "w_rate": draw_w_rate(jax.random.fold_in(arg_keys[14], 71), 0),
        "conv_w": gaussian(arg_keys[5], (TAPS, H, 2 * DK + DV), TAPS ** -0.5, 3.0, ((1, 4),)),
        "a_log": draw_a_log(jax.random.fold_in(arg_keys[14], 71), 0),
        "dt_bias": jnp.clip(jax.random.uniform(arg_keys[7], (H,), jnp.float32, -1.0, 1.0) * levels(arg_keys[7], (H,), ((0, 4),), -0.4, 0.0), -1.0, 1.0),
        "out_gain": jnp.clip(1.0 + 0.15 * jax.random.normal(arg_keys[8], (DV,), jnp.float32), 0.25, 1.75).astype(jnp.bfloat16),
        "w_out": gaussian(arg_keys[9], (D, H, DV), (H * DV // 4) ** -0.5, 0.1875, ((1, 4),)),
        "norm2_gain": jnp.clip(1.0 + 0.15 * jax.random.normal(arg_keys[10], (D,), jnp.float32), 0.25, 1.75).astype(jnp.bfloat16),
        "w_up": gaussian(arg_keys[11], (D, 2, FF), D ** -0.5, 0.125, ((2, 4),)),
        "w_down": gaussian(arg_keys[12], (D, FF), (FF // 4) ** -0.5, 0.15625, ((1, 4),)),
        "cotangent": gaussian(arg_keys[13], (TOKENS, D), 1.0, 6.0, ((0, 8),)),
    }


EPSILON = 1e-06
EXACT_ARITHMETIC = lax.Precision.HIGHEST

@jax.custom_vjp
def low(v):
    return lax.optimization_barrier(v.astype(jnp.bfloat16)).astype(jnp.float32)

@jax.custom_vjp
def low_back(v):
    return v

def low_keep(v):
    return (low(v), None)

def low_pass(kept, grad):
    return (grad,)

def back_keep(v):
    return (v, None)

def reverse_lower_triangle(kept, grad):
    return (low(grad),)
low.defvjp(low_keep, low_pass)
low_back.defvjp(back_keep, reverse_lower_triangle)

def norm_scale(values):
    return lax.rsqrt(lax.optimization_barrier(jnp.mean(values * values, axis=-1, keepdims=True)) + EPSILON)

def unit_rows(values):
    return values * lax.rsqrt(lax.optimization_barrier(jnp.sum(values * values, axis=-1, keepdims=True)) + EPSILON)

def short_conv(conv_rows, weights, seg_ids):
    summed = weights[TAPS - 1] * conv_rows
    for offset in range(1, TAPS):
        moved = jnp.concatenate([jnp.zeros((offset,) + conv_rows.shape[1:], conv_rows.dtype), conv_rows[:-offset]], axis=0)
        moved_ids = jnp.concatenate([jnp.full((offset,), -1, jnp.int32), seg_ids[:-offset]])
        keeping = (moved_ids == seg_ids).astype(conv_rows.dtype)
        summed = summed + weights[TAPS - 1 - offset] * moved * keeping[:, None, None]
    return summed

def delta_rule(query, keys, values, strength, retain):

    def advance(carried_state, inputs):
        single_query_row, single_key_row, value_row, strength_row, retain_row = inputs
        projected_values = jnp.einsum('fg,fgm->fm', single_key_row, carried_state, precision=EXACT_ARITHMETIC)
        update = value_row - retain_row[:, None] * projected_values
        carried_state = retain_row[:, None, None] * carried_state + (strength_row[:, None] * single_key_row)[:, :, None] * update[:, None, :]
        return (carried_state, jnp.einsum('fg,fgm->fm', single_query_row, carried_state, precision=EXACT_ARITHMETIC))

    def one_block(carried_state, inputs):
        return lax.scan(advance, carried_state, inputs)
    number_of_segments = TOKENS // GROUP
    shaped = tuple((array.reshape((number_of_segments, GROUP) + array.shape[1:]) for array in (query, keys, values, strength, retain)))
    initial = jnp.zeros((H, DK, DV), query.dtype)
    unused, emitted = lax.scan(jax.checkpoint(one_block), initial, shaped)
    return emitted.reshape(TOKENS, H, DV)

def layer(tokens_f, gain_one, mix_w, rate_w, conv_f, log_rate, offset_learning_speed, gain_out, out_w, gain_two, up_w, down_w, seg_ids, resets):
    normed_one = low(tokens_f * norm_scale(tokens_f) * gain_one)
    mixed = low_back(jnp.einsum('td,dhc->thc', normed_one, mix_w, precision=EXACT_ARITHMETIC))
    rate_rows = low_back(jnp.einsum('td,dhc->thc', normed_one, rate_w, precision=EXACT_ARITHMETIC))
    conv_rows = low(mixed[..., :2 * DK + DV])
    gate_rows = mixed[..., 2 * DK + DV:]
    active = jax.nn.silu(short_conv(conv_rows, conv_f, seg_ids))
    query = low(unit_rows(active[..., :DK]))
    keys = low(unit_rows(active[..., DK:2 * DK]))
    values = low(active[..., 2 * DK:])
    strength = jax.nn.sigmoid(rate_rows[..., 1])
    log_decay = -jnp.exp(log_rate) * jax.nn.softplus(rate_rows[..., 0] + offset_learning_speed)
    retain = jnp.exp(log_decay) * (1.0 - resets)[:, None]
    core_output = delta_rule(query * DK ** (-0.5), keys, values, strength, retain)
    normed_out = low(core_output * norm_scale(core_output) * gain_out * jax.nn.silu(gate_rows))
    mixer_out = low_back(jnp.einsum('thv,dhv->td', normed_out, out_w, precision=EXACT_ARITHMETIC))
    residual = tokens_f + mixer_out
    normed_two = low(residual * norm_scale(residual) * gain_two)
    gate_up = low_back(jnp.einsum('td,dcf->tcf', normed_two, up_w, precision=EXACT_ARITHMETIC))
    hidden = low(jax.nn.silu(gate_up[:, 0]) * gate_up[:, 1])
    return residual + jnp.einsum('tf,df->td', hidden, down_w, precision=EXACT_ARITHMETIC)

def reference(tokens, seg_ids, norm1_gain, w_mix, w_rate, conv_w, a_log, dt_bias, out_gain, w_out, norm2_gain, w_up, w_down, cotangent):
    changed = (seg_ids[1:] != seg_ids[:-1]).astype(jnp.float32)
    resets = jnp.concatenate([jnp.zeros((1,), jnp.float32), changed])

    def forward(tokens_f, gain_one, mix_w, rate_w, conv_f, log_rate, offset_learning_speed, gain_out, out_w, gain_two, up_w, down_w):
        return layer(tokens_f, gain_one, mix_w, rate_w, conv_f, log_rate, offset_learning_speed, gain_out, out_w, gain_two, up_w, down_w, seg_ids, resets)
    primals = tuple((array.astype(jnp.float32) for array in (tokens, norm1_gain, w_mix, w_rate, conv_w, a_log, dt_bias, out_gain, w_out, norm2_gain, w_up, w_down)))
    layer_out, pullback = jax.vjp(forward, *primals)
    gradients = pullback(cotangent.astype(jnp.float32))
    return (layer_out.astype(jnp.bfloat16), gradients[0].astype(jnp.bfloat16), gradients[1], gradients[2], gradients[3], gradients[4], gradients[5], gradients[6], gradients[7], gradients[8], gradients[9], gradients[10], gradients[11])
```

```python
import jax
import jax.numpy as jnp
from jax import lax
from jax.sharding import PartitionSpec as P

DK = 128
GROUP = 64


EPSILON = 1e-06
EXACT_ARITHMETIC = lax.Precision.HIGHEST
FAST_ARITHMETIC = lax.Precision.HIGH


def shifted(block, axis, distance):
    devices = range(lax.axis_size(axis))
    route = [(i - distance, i) for i in devices if i - distance in devices]
    return lax.ppermute(block, axis, route)


def carried_in(value, axis, join, neutral):
    place = lax.axis_index(axis)
    gathered = jax.tree.map(
        lambda a, kind: lax.all_gather(a.astype(kind), axis), value, (jnp.bfloat16, jnp.bfloat16)
    )
    state = jax.tree.map(lambda a, e: jnp.zeros_like(a) + jnp.asarray(e, a.dtype), value, neutral)

    def one(lap, state):
        return join(
            state,
            jax.tree.map(
                lambda a, own: lax.dynamic_index_in_dim(a, lap, 0, False).astype(own.dtype),
                gathered,
                value,
            ),
        )

    return lax.fori_loop(0, place, one, state)


def carried_in_2(value, axis, join, neutral):
    count, mine = (lax.axis_size(axis), lax.axis_index(axis))
    pieces = jax.tree.map(lambda part: lax.all_gather(part, axis), value)
    pieces = jax.tree.map(lambda part: part[::-1], pieces)
    mine = count - 1 - mine
    running = jax.tree.map(
        lambda part, zero: jnp.full_like(part, 0) + jnp.asarray(zero, part.dtype), value, neutral
    )

    def lap(position, running):
        longer = join(running, jax.tree.map(lambda part: part[position], pieces))
        return jax.tree.map(lambda new, old: jnp.where(position < mine, new, old), longer, running)

    return lax.fori_loop(0, count - 1, lap, running)


def rounded(values):
    return values.astype(jnp.bfloat16).astype(jnp.float32)


def norm_scale(values):
    return lax.rsqrt(jnp.mean(values * values, axis=-1, keepdims=True) + EPSILON)


def unit_rows(values):
    return values * lax.rsqrt(jnp.sum(values * values, axis=-1, keepdims=True) + EPSILON)


def norm_back(grad_normed, gain_f, x_hat, scales):
    shaped = grad_normed * gain_f
    return scales * (shaped - x_hat * jnp.mean(shaped * x_hat, axis=-1, keepdims=True))


def conv_features(padded, weights, keeping):
    taps_all = weights.shape[0]
    length = keeping.shape[1]
    summed = weights[taps_all - 1] * padded[taps_all - 1 :]
    for offset in range(1, taps_all):
        begin_at = taps_all - 1 - offset
        summed = (
            summed
            + weights[begin_at]
            * padded[begin_at : begin_at + length]
            * keeping[offset - 1][:, None, None]
        )
    active = jax.nn.silu(summed)
    return (unit_rows(active[..., :DK]), unit_rows(active[..., DK : 2 * DK]), active[..., 2 * DK :])


def rate_terms(rate_rows, a_log, dt_bias):
    strength = jax.nn.sigmoid(rate_rows[..., 1])
    log_decay = -jnp.exp(a_log) * jax.nn.softplus(rate_rows[..., 0] + dt_bias)
    return (strength, log_decay)


def gated_norm(core_rows, gate_rows, gain_rows):
    return core_rows * norm_scale(core_rows) * gain_rows * jax.nn.silu(gate_rows)


def swiglu(gate_up):
    return jax.nn.silu(gate_up[:, 0]) * gate_up[:, 1]


def batched_mm(left_mat, right_mat):
    return jnp.einsum("hij,hjk->hik", left_mat, right_mat, precision=FAST_ARITHMETIC)


def compose(earlier, later):
    return (batched_mm(later[0], earlier[0]), batched_mm(later[0], earlier[1]) + later[1])


def unit_lower_inverse(lower_mat):
    size = lower_mat.shape[-1]
    rows = lax.broadcasted_iota(jnp.int32, (size, size), 0)
    cols = lax.broadcasted_iota(jnp.int32, (size, size), 1)
    eye = (rows == cols).astype(lower_mat.dtype)
    strict = lower_mat - eye
    inverse = eye
    width = 1
    while width < size:
        within = ((rows // (2 * width)) == (cols // (2 * width))) & (
            (rows // width) != (cols // width)
        )
        off = strict * within.astype(lower_mat.dtype)
        if width == 1:
            inverse = eye - off
        else:
            inverse = inverse - jnp.einsum(
                "...ij,...jk->...ik",
                inverse,
                jnp.einsum("...ij,...jk->...ik", off, inverse, precision=EXACT_ARITHMETIC),
                precision=EXACT_ARITHMETIC,
            )
        width *= 2
    return inverse


def delta_local(query, keys, values, strength, log_decay, resets):
    length, head_count, key_size = keys.shape
    payload_dimension = values.shape[-1]
    number_of_segments = length // GROUP

    def blocked(array):
        shaped = array.reshape((number_of_segments, GROUP, head_count) + array.shape[2:])
        return jnp.moveaxis(shaped, 2, 1)

    stacked = jnp.concatenate(
        [values, jnp.zeros((length, head_count, key_size), jnp.float32)], axis=-1
    )
    query_b = blocked(query * key_size ** (-0.5))
    keys_b = blocked(keys)
    stacked_b = blocked(stacked)
    strength_b = blocked(strength)
    decay_sum = jnp.cumsum(blocked(log_decay), axis=-1)
    pieces = jnp.cumsum(resets.reshape(number_of_segments, GROUP), axis=-1)
    row_ids = lax.broadcasted_iota(jnp.int32, (GROUP, GROUP), 0)
    col_ids = lax.broadcasted_iota(jnp.int32, (GROUP, GROUP), 1)
    joined = pieces[:, :, None] == pieces[:, None, :]
    inside = (joined & (row_ids >= col_ids))[:, None].astype(jnp.float32)
    before = (joined & (row_ids > col_ids))[:, None].astype(jnp.float32)
    spread = decay_sum[..., :, None] - decay_sum[..., None, :]
    decays = jnp.exp(jnp.where(inside > 0, spread, 0.0)) * inside
    from_start = jnp.exp(decay_sum) * (pieces == 0)[:, None, :].astype(jnp.float32)
    to_end = jnp.exp(decay_sum[..., -1:] - decay_sum) * (pieces == pieces[:, -1:])[
        :, None, :
    ].astype(jnp.float32)
    key_dots = jnp.einsum("nhtk,nhjk->nhtj", keys_b, keys_b, precision=FAST_ARITHMETIC)
    lower_mat = (
        jnp.eye(GROUP, dtype=jnp.float32) + key_dots * decays * before * strength_b[..., :, None]
    )

    inverse = unit_lower_inverse(lower_mat)

    def solved(rhs_rows):
        return jnp.einsum("nhtj,nhjw->nhtw", inverse, rhs_rows, precision=FAST_ARITHMETIC)

    value_part = solved(strength_b[..., None] * stacked_b)
    state_part = solved((strength_b * from_start)[..., None] * keys_b)
    query_keys = jnp.einsum("nhtk,nhjk->nhtj", query_b, keys_b, precision=FAST_ARITHMETIC) * decays
    end_keys = to_end[..., None] * keys_b
    initial = jnp.concatenate(
        [
            jnp.zeros((head_count, key_size, payload_dimension), jnp.float32),
            jnp.broadcast_to(
                jnp.eye(key_size, dtype=jnp.float32), (head_count, key_size, key_size)
            ),
        ],
        axis=-1,
    )

    def advance(carried_state, inputs):
        value_rows, state_rows, query_rows, mixing, end_rows, start_decay, block_decay = inputs
        new_values = value_rows - jnp.einsum(
            "htk,hkw->htw", state_rows, carried_state, precision=FAST_ARITHMETIC
        )
        emitted = start_decay[..., None] * jnp.einsum(
            "htk,hkw->htw", query_rows, carried_state, precision=FAST_ARITHMETIC
        ) + jnp.einsum("htj,hjw->htw", mixing, new_values, precision=FAST_ARITHMETIC)
        carried_state = block_decay[:, None, None] * carried_state + jnp.einsum(
            "hjk,hjw->hkw", end_rows, new_values, precision=FAST_ARITHMETIC
        )
        return (carried_state, emitted)

    final_state, emitted_all = lax.scan(
        advance,
        initial,
        (value_part, state_part, query_b, query_keys, end_keys, from_start, from_start[..., -1]),
    )
    emitted_all = jnp.moveaxis(emitted_all, 1, 2).reshape(
        length, head_count, payload_dimension + key_size
    )
    return (
        emitted_all[..., :payload_dimension],
        emitted_all[..., payload_dimension:],
        final_state[..., :payload_dimension],
        final_state[..., payload_dimension:],
    )


def shards(
    tokens,
    seg_ids,
    norm1_gain,
    w_mix,
    w_rate,
    conv_w,
    a_log,
    dt_bias,
    out_gain,
    w_out,
    norm2_gain,
    w_up,
    w_down,
    cotangent,
):
    length = tokens.shape[0]
    head_count = w_mix.shape[1]
    taps_all = conv_w.shape[0]
    rim_rows = taps_all - 1
    conv_width = conv_w.shape[2]
    tp_index = lax.axis_index("tp")
    tokens_f = tokens.astype(jnp.float32)
    gain_one = norm1_gain.astype(jnp.float32)
    scale_one = norm_scale(tokens_f)
    x_hat_one = tokens_f * scale_one
    normed_one = (x_hat_one * gain_one).astype(jnp.bfloat16)
    mixed = jnp.einsum("td,dhc->thc", normed_one, w_mix, preferred_element_type=jnp.float32)
    rate_rows = jnp.einsum("td,dhc->thc", normed_one, w_rate, preferred_element_type=jnp.float32)
    conv_rows = mixed[..., :conv_width].astype(jnp.bfloat16)
    gate_rows = mixed[..., conv_width:]
    tail_rows, tail_ids = shifted(
        (conv_rows[length - rim_rows :], seg_ids[length - rim_rows :].astype(jnp.bfloat16)),
        "seq",
        1,
    )
    own_ids = seg_ids.astype(jnp.float32)
    padded_ids = jnp.concatenate([tail_ids.astype(jnp.float32), own_ids])
    keeping = jnp.stack(
        [
            (padded_ids[rim_rows - offset : rim_rows - offset + length] == own_ids).astype(
                jnp.float32
            )
            for offset in range(1, taps_all)
        ]
    )
    resets = (padded_ids[rim_rows - 1 : rim_rows - 1 + length] != own_ids).astype(jnp.float32)
    padded = jnp.concatenate([tail_rows, conv_rows]).astype(jnp.float32)
    features, conv_pull = jax.vjp(
        lambda padded_rows, weights: conv_features(padded_rows, weights, keeping),
        padded,
        conv_w.astype(jnp.float32),
    )
    query = rounded(features[0])
    keys = rounded(features[1])
    values = rounded(features[2])
    (strength, log_decay), rate_pull = jax.vjp(rate_terms, rate_rows, a_log, dt_bias)
    (local_output, probe_destinations, base_state, transfer), delta_pull = jax.vjp(
        lambda q, k, v, b, g: delta_local(q, k, v, b, g, resets),
        query,
        keys,
        values,
        strength,
        log_decay,
    )
    zero_state = jnp.zeros_like(base_state)
    identity_mats = jnp.broadcast_to(jnp.eye(transfer.shape[1], dtype=jnp.float32), transfer.shape)
    entering_memory_matrix = carried_in(
        (transfer, base_state), "seq", compose, (identity_mats, zero_state)
    )[1]
    core_output = local_output + jnp.einsum(
        "vkq,kqp->vkp", probe_destinations, entering_memory_matrix, precision=FAST_ARITHMETIC
    )
    normed_out_f, gate_pull = jax.vjp(
        gated_norm, core_output, gate_rows, out_gain.astype(jnp.float32)
    )
    normed_out = normed_out_f.astype(jnp.bfloat16)
    mixer_part = jnp.einsum("thv,dhv->td", normed_out, w_out, preferred_element_type=jnp.float32)
    gain_two = norm2_gain.astype(jnp.float32)
    residual = tokens_f + lax.psum(mixer_part.astype(jnp.bfloat16), "tp").astype(jnp.float32)
    scale_two = norm_scale(residual)
    x_hat_two = residual * scale_two
    normed_two = (x_hat_two * gain_two).astype(jnp.bfloat16)
    gate_up = jnp.einsum("td,dcf->tcf", normed_two, w_up, preferred_element_type=jnp.float32)
    hidden_f, hidden_pull = jax.vjp(swiglu, gate_up)
    hidden = hidden_f.astype(jnp.bfloat16)
    ffn_part = jnp.einsum("tf,df->td", hidden, w_down, preferred_element_type=jnp.float32)
    grad_down = jnp.einsum("tf,td->df", hidden, cotangent, preferred_element_type=jnp.float32)
    grad_hidden = jnp.einsum("td,df->tf", cotangent, w_down, preferred_element_type=jnp.float32)
    grad_gate_up = hidden_pull(grad_hidden)[0].astype(jnp.bfloat16)
    grad_up = jnp.einsum(
        "td,tcf->dcf", normed_two, grad_gate_up, preferred_element_type=jnp.float32
    )
    ffn_in_part = jnp.einsum("tcf,dcf->td", grad_gate_up, w_up, preferred_element_type=jnp.float32)
    ffn_in = lax.psum(ffn_in_part.astype(jnp.bfloat16), "tp").astype(jnp.float32)
    gain_two_grad = jnp.sum(ffn_in_part * x_hat_two, axis=0)
    grad_residual = cotangent.astype(jnp.float32) + norm_back(
        ffn_in, gain_two, x_hat_two, scale_two
    )
    grad_mixer = grad_residual.astype(jnp.bfloat16)
    grad_w_out = jnp.einsum(
        "td,thv->dhv", grad_mixer, normed_out, preferred_element_type=jnp.float32
    )
    grad_normed_out = jnp.einsum(
        "td,dhv->thv", grad_mixer, w_out, preferred_element_type=jnp.float32
    )
    core_output_grad, grad_gate_rows, out_gain_grad = gate_pull(grad_normed_out)
    own_state_gradient = jnp.einsum(
        "eyc,eyn->ycn", probe_destinations, core_output_grad, precision=FAST_ARITHMETIC
    )
    transfer_t = jnp.swapaxes(transfer, 1, 2)
    state_gradient = carried_in_2(
        (transfer_t, own_state_gradient), "seq", compose, (identity_mats, zero_state)
    )[1]
    branch_derivatives = jnp.einsum(
        "xao,aeo->xae", core_output_grad, entering_memory_matrix, precision=FAST_ARITHMETIC
    )
    transfer_gradient = jnp.einsum(
        "zne,zye->zny", state_gradient, entering_memory_matrix, precision=FAST_ARITHMETIC
    )
    ffn_send, early_send, state_gradient = lax.optimization_barrier(
        (
            ffn_part.astype(jnp.bfloat16),
            tuple(part.astype(jnp.bfloat16) for part in (grad_w_out, grad_up, grad_down)),
            state_gradient,
        )
    )
    ffn_sum = lax.psum(ffn_send, "tp")
    early_sums = tuple(
        lax.psum_scatter(part, "seq", scatter_dimension=0, tiled=True) for part in early_send
    )
    delta_grads = delta_pull(
        (core_output_grad, branch_derivatives, state_gradient, transfer_gradient)
    )
    ffn_sum, early_sums, delta_grads = lax.optimization_barrier(
        (ffn_sum, early_sums, delta_grads)
    )
    grad_query, grad_keys, grad_values, grad_strength, grad_decay = delta_grads
    layer_out = (residual + ffn_sum.astype(jnp.float32)).astype(jnp.bfloat16)
    grad_rate_rows, a_log_grad, dt_bias_grad = rate_pull((grad_strength, grad_decay))
    grad_padded, conv_grad = conv_pull((grad_query, grad_keys, grad_values))
    back_rows = shifted(grad_padded[:rim_rows], "seq", -1)
    grad_conv_rows = grad_padded[rim_rows:] + jnp.concatenate(
        [jnp.zeros((length - rim_rows,) + back_rows.shape[1:], jnp.float32), back_rows]
    )
    grad_mixed = jnp.concatenate([grad_conv_rows, grad_gate_rows], axis=-1).astype(jnp.bfloat16)
    grad_rates = grad_rate_rows.astype(jnp.bfloat16)
    grad_mix = jnp.einsum("td,thc->dhc", normed_one, grad_mixed, preferred_element_type=jnp.float32)
    grad_rate = jnp.einsum(
        "td,thc->dhc", normed_one, grad_rates, preferred_element_type=jnp.float32
    )
    mixer_in_part = jnp.einsum(
        "thc,dhc->td", grad_mixed, w_mix, preferred_element_type=jnp.float32
    ) + jnp.einsum("thc,dhc->td", grad_rates, w_rate, preferred_element_type=jnp.float32)
    mixer_in = lax.psum(mixer_in_part.astype(jnp.bfloat16), "tp").astype(jnp.float32)
    gain_one_grad = jnp.sum(mixer_in_part * x_hat_one, axis=0)
    grad_tokens = (grad_residual + norm_back(mixer_in, gain_one, x_hat_one, scale_one)).astype(
        jnp.bfloat16
    )
    total_heads = head_count * lax.axis_size("tp")
    head_start = tp_index * head_count
    zero_index = tp_index * 0
    conv_full = lax.dynamic_update_slice(
        jnp.zeros((taps_all, total_heads, conv_width), jnp.float32),
        conv_grad,
        (zero_index, head_start, zero_index),
    )
    a_log_full = lax.dynamic_update_slice(
        jnp.zeros((total_heads,), jnp.float32), a_log_grad, (head_start,)
    )
    dt_bias_full = lax.dynamic_update_slice(
        jnp.zeros((total_heads,), jnp.float32), dt_bias_grad, (head_start,)
    )
    small_parts = (gain_one_grad, gain_two_grad, out_gain_grad, conv_full, a_log_full, dt_bias_full)
    small_flat = lax.psum(
        jnp.concatenate([part.reshape(-1) for part in small_parts]), ("seq", "tp")
    )
    small_sums = []
    start_at = 0
    for part in small_parts:
        small_sums.append(small_flat[start_at : start_at + part.size].reshape(part.shape))
        start_at += part.size
    weight_sums = (
        lax.psum_scatter(
            grad_mix.astype(jnp.bfloat16), "seq", scatter_dimension=0, tiled=True
        ).astype(jnp.float32),
        lax.psum_scatter(
            grad_rate.astype(jnp.bfloat16), "seq", scatter_dimension=0, tiled=True
        ).astype(jnp.float32),
        early_sums[0].astype(jnp.float32),
        early_sums[1].astype(jnp.float32),
        early_sums[2].astype(jnp.float32),
    )
    return (
        layer_out,
        grad_tokens,
        small_sums[0],
        weight_sums[0],
        weight_sums[1],
        small_sums[3],
        small_sums[4],
        small_sums[5],
        small_sums[2],
        weight_sums[2],
        small_sums[1],
        weight_sums[3],
        weight_sums[4],
    )


def solution(mesh):
    in_specs = (
        P("seq", None),
        P("seq"),
        P(),
        P(None, "tp", None),
        P(None, "tp", None),
        P(None, "tp", None),
        P("tp"),
        P("tp"),
        P(),
        P(None, "tp", None),
        P(),
        P(None, None, "tp"),
        P(None, "tp"),
        P("seq", None),
    )
    out_specs = (
        P("seq", None),
        P("seq", None),
        P(),
        P("seq", "tp", None),
        P("seq", "tp", None),
        P(),
        P(),
        P(),
        P(),
        P("seq", "tp", None),
        P(),
        P("seq", None, "tp"),
        P("seq", "tp"),
    )
    return jax.shard_map(shards, mesh=mesh, in_specs=in_specs, out_specs=out_specs, check_vma=False)
```

```python
import functools

import jax
import jax.numpy as jnp
from jax import lax
from jax.experimental import pallas as pl
from jax.experimental.pallas import tpu as pltpu
from jax.sharding import PartitionSpec as P

MESH_IDS = pl.DeviceIdType.MESH

DK = 128
GROUP = 64


EPSILON = 1e-06
EXACT_ARITHMETIC = lax.Precision.HIGHEST
FAST_ARITHMETIC = lax.Precision.HIGH


def shifted(block, axis, distance):
    devices = range(lax.axis_size(axis))
    route = [(i - distance, i) for i in devices if i - distance in devices]
    return lax.ppermute(block, axis, route)


def peer_gather_kernel(axis, count, mode, x_ref, out_ref, send_sem, recv_sem):
    me = lax.axis_index(axis)
    barrier = pltpu.get_barrier_semaphore()
    for step in range(1, count):
        pl.semaphore_signal(
            barrier, inc=1, device_id={axis: lax.rem(me + step, count)}, device_id_type=MESH_IDS
        )
    pl.semaphore_wait(barrier, count - 1)

    def link(step, source, target):
        return pltpu.make_async_remote_copy(
            src_ref=x_ref,
            dst_ref=out_ref.at[source],
            send_sem=send_sem.at[step],
            recv_sem=recv_sem.at[step],
            device_id={axis: target},
            device_id_type=MESH_IDS,
        )

    def target_of(step):
        if mode == "up":
            return me + step, me + step < count
        if mode == "down":
            return me - step, me - step >= 0
        return lax.rem(me + step, count), me >= 0

    def source_of(step):
        if mode == "up":
            return me - step, me - step >= 0
        if mode == "down":
            return me + step, me + step < count
        return lax.rem(me + count - step, count), me >= 0

    for step in range(1, count):
        target, sending = target_of(step)

        @pl.when(sending)
        def _():
            link(step, me, target).start()

    for step in range(1, count):
        target, sending = target_of(step)
        source, receiving = source_of(step)

        @pl.when(sending)
        def _():
            link(step, me, target).wait_send()

        @pl.when(receiving)
        def _():
            link(step, source, source).wait_recv()


def peer_gather(x, axis, mode, collective_id):
    count = lax.axis_size(axis)
    return pl.pallas_call(
        functools.partial(peer_gather_kernel, axis, count, mode),
        out_shape=jax.ShapeDtypeStruct((count,) + x.shape, x.dtype),
        in_specs=[pl.BlockSpec(memory_space=pl.ANY)],
        out_specs=pl.BlockSpec(memory_space=pl.ANY),
        scratch_shapes=[pltpu.SemaphoreType.DMA((count,)), pltpu.SemaphoreType.DMA((count,))],
        compiler_params=pltpu.CompilerParams(collective_id=collective_id, has_side_effects=True),
    )(x)


def joined_gather(value, axis, mode, collective_id, kind):
    widths = [part.shape[-1] for part in value]
    packed = jnp.concatenate([part.astype(kind) for part in value], axis=-1)
    gathered = peer_gather(packed, axis, mode, collective_id)
    pieces = []
    start_at = 0
    for width in widths:
        pieces.append(gathered[..., start_at : start_at + width])
        start_at += width
    return tuple(pieces)


def carried_in(value, axis, join, neutral):
    place = lax.axis_index(axis)
    gathered = joined_gather(value, axis, "up", 1, jnp.bfloat16)
    state = jax.tree.map(lambda a, e: jnp.zeros_like(a) + jnp.asarray(e, a.dtype), value, neutral)

    def one(lap, state):
        return join(
            state,
            jax.tree.map(
                lambda a, own: lax.dynamic_index_in_dim(a, lap, 0, False).astype(own.dtype),
                gathered,
                value,
            ),
        )

    return lax.fori_loop(0, place, one, state)


def carried_in_2(value, axis, join, neutral):
    count, mine = (lax.axis_size(axis), lax.axis_index(axis))
    pieces = jax.tree.map(lambda part: lax.all_gather(part, axis), value)
    pieces = jax.tree.map(lambda part: part[::-1], pieces)
    mine = count - 1 - mine
    running = jax.tree.map(
        lambda part, zero: jnp.full_like(part, 0) + jnp.asarray(zero, part.dtype), value, neutral
    )

    def lap(position, running):
        longer = join(running, jax.tree.map(lambda part: part[position], pieces))
        return jax.tree.map(lambda new, old: jnp.where(position < mine, new, old), longer, running)

    return lax.fori_loop(0, count - 1, lap, running)


def own_then_peers(flat, axis, collective_id):
    size = flat.shape[0]
    padded = -(-size // 1024) * 1024
    tiles = jnp.pad(flat, (0, padded - size)).reshape(padded // 128, 128)
    gathered = peer_gather(tiles, axis, "all", collective_id)
    slots = lax.broadcasted_iota(jnp.int32, gathered.shape, 0)
    filled = jnp.where(slots == lax.axis_index(axis), tiles[None], gathered)
    return filled.reshape(gathered.shape[0], padded)[:, :size]


def rounded(values):
    return values.astype(jnp.bfloat16).astype(jnp.float32)


def norm_scale(values):
    return lax.rsqrt(jnp.mean(values * values, axis=-1, keepdims=True) + EPSILON)


def unit_rows(values):
    return values * lax.rsqrt(jnp.sum(values * values, axis=-1, keepdims=True) + EPSILON)


def norm_back(grad_normed, gain_f, x_hat, scales):
    shaped = grad_normed * gain_f
    return scales * (shaped - x_hat * jnp.mean(shaped * x_hat, axis=-1, keepdims=True))


def conv_features(padded, weights, keeping):
    taps_all = weights.shape[0]
    length = keeping.shape[1]
    summed = weights[taps_all - 1] * padded[taps_all - 1 :]
    for offset in range(1, taps_all):
        begin_at = taps_all - 1 - offset
        summed = (
            summed
            + weights[begin_at]
            * padded[begin_at : begin_at + length]
            * keeping[offset - 1][:, None, None]
        )
    active = jax.nn.silu(summed)
    return (unit_rows(active[..., :DK]), unit_rows(active[..., DK : 2 * DK]), active[..., 2 * DK :])


def rate_terms(rate_rows, a_log, dt_bias):
    strength = jax.nn.sigmoid(rate_rows[..., 1])
    log_decay = -jnp.exp(a_log) * jax.nn.softplus(rate_rows[..., 0] + dt_bias)
    return (strength, log_decay)


def gated_norm(core_rows, gate_rows, gain_rows):
    return core_rows * norm_scale(core_rows) * gain_rows * jax.nn.silu(gate_rows)


def swiglu(gate_up):
    return jax.nn.silu(gate_up[:, 0]) * gate_up[:, 1]


def batched_mm(left_mat, right_mat):
    return jnp.einsum("hij,hjk->hik", left_mat, right_mat, precision=FAST_ARITHMETIC)


def compose(earlier, later):
    return (batched_mm(later[0], earlier[0]), batched_mm(later[0], earlier[1]) + later[1])


def unit_lower_inverse(lower_mat):
    size = lower_mat.shape[-1]
    rows = lax.broadcasted_iota(jnp.int32, (size, size), 0)
    cols = lax.broadcasted_iota(jnp.int32, (size, size), 1)
    eye = (rows == cols).astype(lower_mat.dtype)
    strict = lower_mat - eye
    inverse = eye
    width = 1
    while width < size:
        within = ((rows // (2 * width)) == (cols // (2 * width))) & (
            (rows // width) != (cols // width)
        )
        off = strict * within.astype(lower_mat.dtype)
        if width == 1:
            inverse = eye - off
        else:
            inverse = inverse - jnp.einsum(
                "...ij,...jk->...ik",
                inverse,
                jnp.einsum("...ij,...jk->...ik", off, inverse, precision=EXACT_ARITHMETIC),
                precision=EXACT_ARITHMETIC,
            )
        width *= 2
    return inverse


def delta_local(query, keys, values, strength, log_decay, resets):
    length, head_count, key_size = keys.shape
    payload_dimension = values.shape[-1]
    number_of_segments = length // GROUP

    def blocked(array):
        shaped = array.reshape((number_of_segments, GROUP, head_count) + array.shape[2:])
        return jnp.moveaxis(shaped, 2, 1)

    stacked = jnp.concatenate(
        [values, jnp.zeros((length, head_count, key_size), jnp.float32)], axis=-1
    )
    query_b = blocked(query * key_size ** (-0.5))
    keys_b = blocked(keys)
    stacked_b = blocked(stacked)
    strength_b = blocked(strength)
    decay_sum = jnp.cumsum(blocked(log_decay), axis=-1)
    pieces = jnp.cumsum(resets.reshape(number_of_segments, GROUP), axis=-1)
    row_ids = lax.broadcasted_iota(jnp.int32, (GROUP, GROUP), 0)
    col_ids = lax.broadcasted_iota(jnp.int32, (GROUP, GROUP), 1)
    joined = pieces[:, :, None] == pieces[:, None, :]
    inside = (joined & (row_ids >= col_ids))[:, None].astype(jnp.float32)
    before = (joined & (row_ids > col_ids))[:, None].astype(jnp.float32)
    spread = decay_sum[..., :, None] - decay_sum[..., None, :]
    decays = jnp.exp(jnp.where(inside > 0, spread, 0.0)) * inside
    from_start = jnp.exp(decay_sum) * (pieces == 0)[:, None, :].astype(jnp.float32)
    to_end = jnp.exp(decay_sum[..., -1:] - decay_sum) * (pieces == pieces[:, -1:])[
        :, None, :
    ].astype(jnp.float32)
    key_dots = jnp.einsum("nhtk,nhjk->nhtj", keys_b, keys_b, precision=FAST_ARITHMETIC)
    lower_mat = (
        jnp.eye(GROUP, dtype=jnp.float32) + key_dots * decays * before * strength_b[..., :, None]
    )

    inverse = unit_lower_inverse(lower_mat)

    def solved(rhs_rows):
        return jnp.einsum("nhtj,nhjw->nhtw", inverse, rhs_rows, precision=FAST_ARITHMETIC)

    value_part = solved(strength_b[..., None] * stacked_b)
    state_part = solved((strength_b * from_start)[..., None] * keys_b)
    query_keys = jnp.einsum("nhtk,nhjk->nhtj", query_b, keys_b, precision=FAST_ARITHMETIC) * decays
    end_keys = to_end[..., None] * keys_b
    initial = jnp.concatenate(
        [
            jnp.zeros((head_count, key_size, payload_dimension), jnp.float32),
            jnp.broadcast_to(
                jnp.eye(key_size, dtype=jnp.float32), (head_count, key_size, key_size)
            ),
        ],
        axis=-1,
    )

    def advance(carried_state, inputs):
        value_rows, state_rows, query_rows, mixing, end_rows, start_decay, block_decay = inputs
        new_values = value_rows - jnp.einsum(
            "htk,hkw->htw", state_rows, carried_state, precision=FAST_ARITHMETIC
        )
        emitted = start_decay[..., None] * jnp.einsum(
            "htk,hkw->htw", query_rows, carried_state, precision=FAST_ARITHMETIC
        ) + jnp.einsum("htj,hjw->htw", mixing, new_values, precision=FAST_ARITHMETIC)
        carried_state = block_decay[:, None, None] * carried_state + jnp.einsum(
            "hjk,hjw->hkw", end_rows, new_values, precision=FAST_ARITHMETIC
        )
        return (carried_state, emitted)

    final_state, emitted_all = lax.scan(
        advance,
        initial,
        (value_part, state_part, query_b, query_keys, end_keys, from_start, from_start[..., -1]),
    )
    emitted_all = jnp.moveaxis(emitted_all, 1, 2).reshape(
        length, head_count, payload_dimension + key_size
    )
    return (
        emitted_all[..., :payload_dimension],
        emitted_all[..., payload_dimension:],
        final_state[..., :payload_dimension],
        final_state[..., payload_dimension:],
    )


def shards(
    tokens,
    seg_ids,
    norm1_gain,
    w_mix,
    w_rate,
    conv_w,
    a_log,
    dt_bias,
    out_gain,
    w_out,
    norm2_gain,
    w_up,
    w_down,
    cotangent,
):
    length = tokens.shape[0]
    head_count = w_mix.shape[1]
    taps_all = conv_w.shape[0]
    rim_rows = taps_all - 1
    conv_width = conv_w.shape[2]
    tp_index = lax.axis_index("tp")
    tokens_f = tokens.astype(jnp.float32)
    gain_one = norm1_gain.astype(jnp.float32)
    scale_one = norm_scale(tokens_f)
    x_hat_one = tokens_f * scale_one
    normed_one = (x_hat_one * gain_one).astype(jnp.bfloat16)
    mixed = jnp.einsum("td,dhc->thc", normed_one, w_mix, preferred_element_type=jnp.float32)
    rate_rows = jnp.einsum("td,dhc->thc", normed_one, w_rate, preferred_element_type=jnp.float32)
    conv_rows = mixed[..., :conv_width].astype(jnp.bfloat16)
    gate_rows = mixed[..., conv_width:]
    tail_rows, tail_ids = shifted(
        (conv_rows[length - rim_rows :], seg_ids[length - rim_rows :].astype(jnp.bfloat16)),
        "seq",
        1,
    )
    own_ids = seg_ids.astype(jnp.float32)
    padded_ids = jnp.concatenate([tail_ids.astype(jnp.float32), own_ids])
    keeping = jnp.stack(
        [
            (padded_ids[rim_rows - offset : rim_rows - offset + length] == own_ids).astype(
                jnp.float32
            )
            for offset in range(1, taps_all)
        ]
    )
    resets = (padded_ids[rim_rows - 1 : rim_rows - 1 + length] != own_ids).astype(jnp.float32)
    padded = jnp.concatenate([tail_rows, conv_rows]).astype(jnp.float32)
    features, conv_pull = jax.vjp(
        lambda padded_rows, weights: conv_features(padded_rows, weights, keeping),
        padded,
        conv_w.astype(jnp.float32),
    )
    query = rounded(features[0])
    keys = rounded(features[1])
    values = rounded(features[2])
    (strength, log_decay), rate_pull = jax.vjp(rate_terms, rate_rows, a_log, dt_bias)
    (local_output, probe_destinations, base_state, transfer), delta_pull = jax.vjp(
        lambda q, k, v, b, g: delta_local(q, k, v, b, g, resets),
        query,
        keys,
        values,
        strength,
        log_decay,
    )
    zero_state = jnp.zeros_like(base_state)
    identity_mats = jnp.broadcast_to(jnp.eye(transfer.shape[1], dtype=jnp.float32), transfer.shape)
    entering_memory_matrix = carried_in(
        (transfer, base_state), "seq", compose, (identity_mats, zero_state)
    )[1]
    core_output = local_output + jnp.einsum(
        "vkq,kqp->vkp", probe_destinations, entering_memory_matrix, precision=FAST_ARITHMETIC
    )
    normed_out_f, gate_pull = jax.vjp(
        gated_norm, core_output, gate_rows, out_gain.astype(jnp.float32)
    )
    normed_out = normed_out_f.astype(jnp.bfloat16)
    mixer_part = jnp.einsum("thv,dhv->td", normed_out, w_out, preferred_element_type=jnp.float32)
    gain_two = norm2_gain.astype(jnp.float32)
    residual = tokens_f + lax.psum(mixer_part.astype(jnp.bfloat16), "tp").astype(jnp.float32)
    scale_two = norm_scale(residual)
    x_hat_two = residual * scale_two
    normed_two = (x_hat_two * gain_two).astype(jnp.bfloat16)
    gate_up = jnp.einsum("td,dcf->tcf", normed_two, w_up, preferred_element_type=jnp.float32)
    hidden_f, hidden_pull = jax.vjp(swiglu, gate_up)
    hidden = hidden_f.astype(jnp.bfloat16)
    ffn_part = jnp.einsum("tf,df->td", hidden, w_down, preferred_element_type=jnp.float32)
    grad_down = jnp.einsum("tf,td->df", hidden, cotangent, preferred_element_type=jnp.float32)
    grad_hidden = jnp.einsum("td,df->tf", cotangent, w_down, preferred_element_type=jnp.float32)
    grad_gate_up = hidden_pull(grad_hidden)[0].astype(jnp.bfloat16)
    grad_up = jnp.einsum(
        "td,tcf->dcf", normed_two, grad_gate_up, preferred_element_type=jnp.float32
    )
    ffn_in_part = jnp.einsum("tcf,dcf->td", grad_gate_up, w_up, preferred_element_type=jnp.float32)
    ffn_in = lax.psum(ffn_in_part.astype(jnp.bfloat16), "tp").astype(jnp.float32)
    gain_two_grad = jnp.sum(ffn_in_part * x_hat_two, axis=0)
    grad_residual = cotangent.astype(jnp.float32) + norm_back(
        ffn_in, gain_two, x_hat_two, scale_two
    )
    grad_mixer = grad_residual.astype(jnp.bfloat16)
    grad_w_out = jnp.einsum(
        "td,thv->dhv", grad_mixer, normed_out, preferred_element_type=jnp.float32
    )
    grad_normed_out = jnp.einsum(
        "td,dhv->thv", grad_mixer, w_out, preferred_element_type=jnp.float32
    )
    core_output_grad, grad_gate_rows, out_gain_grad = gate_pull(grad_normed_out)
    own_state_gradient = jnp.einsum(
        "eyc,eyn->ycn", probe_destinations, core_output_grad, precision=FAST_ARITHMETIC
    )
    transfer_t = jnp.swapaxes(transfer, 1, 2)
    state_gradient = carried_in_2(
        (transfer_t, own_state_gradient), "seq", compose, (identity_mats, zero_state)
    )[1]
    branch_derivatives = jnp.einsum(
        "xao,aeo->xae", core_output_grad, entering_memory_matrix, precision=FAST_ARITHMETIC
    )
    transfer_gradient = jnp.einsum(
        "zne,zye->zny", state_gradient, entering_memory_matrix, precision=FAST_ARITHMETIC
    )
    ffn_send, early_send, state_gradient = lax.optimization_barrier(
        (
            ffn_part.astype(jnp.bfloat16),
            tuple(part.astype(jnp.bfloat16) for part in (grad_w_out, grad_up, grad_down)),
            state_gradient,
        )
    )
    ffn_sum = lax.psum(ffn_send, "tp")
    early_sums = tuple(
        lax.psum_scatter(part, "seq", scatter_dimension=0, tiled=True) for part in early_send
    )
    delta_grads = delta_pull(
        (core_output_grad, branch_derivatives, state_gradient, transfer_gradient)
    )
    ffn_sum, early_sums, delta_grads = lax.optimization_barrier(
        (ffn_sum, early_sums, delta_grads)
    )
    grad_query, grad_keys, grad_values, grad_strength, grad_decay = delta_grads
    layer_out = (residual + ffn_sum.astype(jnp.float32)).astype(jnp.bfloat16)
    grad_rate_rows, a_log_grad, dt_bias_grad = rate_pull((grad_strength, grad_decay))
    grad_padded, conv_grad = conv_pull((grad_query, grad_keys, grad_values))
    back_rows = shifted(grad_padded[:rim_rows], "seq", -1)
    grad_conv_rows = grad_padded[rim_rows:] + jnp.concatenate(
        [jnp.zeros((length - rim_rows,) + back_rows.shape[1:], jnp.float32), back_rows]
    )
    grad_mixed = jnp.concatenate([grad_conv_rows, grad_gate_rows], axis=-1).astype(jnp.bfloat16)
    grad_rates = grad_rate_rows.astype(jnp.bfloat16)
    grad_mix = jnp.einsum("td,thc->dhc", normed_one, grad_mixed, preferred_element_type=jnp.float32)
    grad_rate = jnp.einsum(
        "td,thc->dhc", normed_one, grad_rates, preferred_element_type=jnp.float32
    )
    mixer_in_part = jnp.einsum(
        "thc,dhc->td", grad_mixed, w_mix, preferred_element_type=jnp.float32
    ) + jnp.einsum("thc,dhc->td", grad_rates, w_rate, preferred_element_type=jnp.float32)
    mixer_in = lax.psum(mixer_in_part.astype(jnp.bfloat16), "tp").astype(jnp.float32)
    gain_one_grad = jnp.sum(mixer_in_part * x_hat_one, axis=0)
    grad_tokens = (grad_residual + norm_back(mixer_in, gain_one, x_hat_one, scale_one)).astype(
        jnp.bfloat16
    )
    seq_index = lax.axis_index("seq")
    tp_count = lax.axis_size("tp")
    seq_parts = (gain_one_grad, gain_two_grad, out_gain_grad, conv_grad, a_log_grad, dt_bias_grad)
    seq_summed = own_then_peers(
        jnp.concatenate([part.reshape(-1) for part in seq_parts] + [grad_rate.reshape(-1)]),
        "seq",
        3,
    )
    seq_summed = jnp.sum(seq_summed, axis=0)
    tp_size = sum(part.size for part in seq_parts)
    rate_rows = grad_rate.shape[0] // lax.axis_size("seq")
    rate_sum = lax.dynamic_slice_in_dim(
        seq_summed[tp_size:].reshape(grad_rate.shape), seq_index * rate_rows, rate_rows, 0
    )
    by_tp = own_then_peers(seq_summed[:tp_size], "tp", 4)
    small_sums = []
    start_at = 0
    for part in seq_parts:
        piece = by_tp[:, start_at : start_at + part.size]
        start_at += part.size
        if part.ndim == 1 and part.shape[0] != head_count:
            small_sums.append(jnp.sum(piece, axis=0))
        elif part.ndim == 1:
            small_sums.append(piece.reshape(tp_count * head_count))
        else:
            small_sums.append(
                jnp.moveaxis(piece.reshape((tp_count,) + part.shape), 0, 1).reshape(
                    (taps_all, tp_count * head_count, conv_width)
                )
            )
    weight_sums = (
        lax.psum_scatter(
            grad_mix.astype(jnp.bfloat16), "seq", scatter_dimension=0, tiled=True
        ).astype(jnp.float32),
        rate_sum,
        early_sums[0].astype(jnp.float32),
        early_sums[1].astype(jnp.float32),
        early_sums[2].astype(jnp.float32),
    )
    return (
        layer_out,
        grad_tokens,
        small_sums[0],
        weight_sums[0],
        weight_sums[1],
        small_sums[3],
        small_sums[4],
        small_sums[5],
        small_sums[2],
        weight_sums[2],
        small_sums[1],
        weight_sums[3],
        weight_sums[4],
    )


def solution(mesh):
    in_specs = (
        P("seq", None),
        P("seq"),
        P(),
        P(None, "tp", None),
        P(None, "tp", None),
        P(None, "tp", None),
        P("tp"),
        P("tp"),
        P(),
        P(None, "tp", None),
        P(),
        P(None, None, "tp"),
        P(None, "tp"),
        P("seq", None),
    )
    out_specs = (
        P("seq", None),
        P("seq", None),
        P(),
        P("seq", "tp", None),
        P("seq", "tp", None),
        P(),
        P(),
        P(),
        P(),
        P("seq", "tp", None),
        P(),
        P("seq", None, "tp"),
        P("seq", "tp"),
    )
    return jax.shard_map(shards, mesh=mesh, in_specs=in_specs, out_specs=out_specs, check_vma=False)
```

```python
import functools

import jax
import jax.numpy as jnp
from jax import lax
from jax.experimental import pallas as pl
from jax.experimental.pallas import tpu as pltpu
from jax.sharding import PartitionSpec as P

MESH_IDS = pl.DeviceIdType.MESH

DK = 128
GROUP = 64


EPSILON = 1e-06
EXACT_ARITHMETIC = lax.Precision.HIGHEST
FAST_ARITHMETIC = lax.Precision.HIGH


def shifted(block, axis, distance):
    devices = range(lax.axis_size(axis))
    route = [(i - distance, i) for i in devices if i - distance in devices]
    return lax.ppermute(block, axis, route)


def peer_gather_kernel(axis, count, mode, x_ref, out_ref, send_sem, recv_sem):
    me = lax.axis_index(axis)
    barrier = pltpu.get_barrier_semaphore()
    for step in range(1, count):
        pl.semaphore_signal(
            barrier, inc=1, device_id={axis: lax.rem(me + step, count)}, device_id_type=MESH_IDS
        )
    pl.semaphore_wait(barrier, count - 1)

    def link(step, source, target):
        return pltpu.make_async_remote_copy(
            src_ref=x_ref,
            dst_ref=out_ref.at[source],
            send_sem=send_sem.at[step],
            recv_sem=recv_sem.at[step],
            device_id={axis: target},
            device_id_type=MESH_IDS,
        )

    def target_of(step):
        if mode == "up":
            return me + step, me + step < count
        if mode == "down":
            return me - step, me - step >= 0
        return lax.rem(me + step, count), me >= 0

    def source_of(step):
        if mode == "up":
            return me - step, me - step >= 0
        if mode == "down":
            return me + step, me + step < count
        return lax.rem(me + count - step, count), me >= 0

    for step in range(1, count):
        target, sending = target_of(step)

        @pl.when(sending)
        def _():
            link(step, me, target).start()

    for step in range(1, count):
        target, sending = target_of(step)
        source, receiving = source_of(step)

        @pl.when(sending)
        def _():
            link(step, me, target).wait_send()

        @pl.when(receiving)
        def _():
            link(step, source, source).wait_recv()


def peer_gather(x, axis, mode, collective_id):
    count = lax.axis_size(axis)
    return pl.pallas_call(
        functools.partial(peer_gather_kernel, axis, count, mode),
        out_shape=jax.ShapeDtypeStruct((count,) + x.shape, x.dtype),
        in_specs=[pl.BlockSpec(memory_space=pl.ANY)],
        out_specs=pl.BlockSpec(memory_space=pl.ANY),
        scratch_shapes=[pltpu.SemaphoreType.DMA((count,)), pltpu.SemaphoreType.DMA((count,))],
        compiler_params=pltpu.CompilerParams(collective_id=collective_id, has_side_effects=True),
    )(x)


def joined_gather(value, axis, mode, collective_id, kind):
    widths = [part.shape[-1] for part in value]
    packed = jnp.concatenate([part.astype(kind) for part in value], axis=-1)
    gathered = peer_gather(packed, axis, mode, collective_id)
    pieces = []
    start_at = 0
    for width in widths:
        pieces.append(gathered[..., start_at : start_at + width])
        start_at += width
    return tuple(pieces)


def carried_in(value, axis, join, neutral):
    place = lax.axis_index(axis)
    gathered = joined_gather(value, axis, "up", 1, jnp.bfloat16)
    state = jax.tree.map(lambda a, e: jnp.zeros_like(a) + jnp.asarray(e, a.dtype), value, neutral)

    def one(lap, state):
        return join(
            state,
            jax.tree.map(
                lambda a, own: lax.dynamic_index_in_dim(a, lap, 0, False).astype(own.dtype),
                gathered,
                value,
            ),
        )

    return lax.fori_loop(0, place, one, state)


def carried_in_2(value, axis, join, neutral):
    count, mine = (lax.axis_size(axis), lax.axis_index(axis))
    pieces = jax.tree.map(lambda part: lax.all_gather(part, axis), value)
    pieces = jax.tree.map(lambda part: part[::-1], pieces)
    mine = count - 1 - mine
    running = jax.tree.map(
        lambda part, zero: jnp.full_like(part, 0) + jnp.asarray(zero, part.dtype), value, neutral
    )

    def lap(position, running):
        longer = join(running, jax.tree.map(lambda part: part[position], pieces))
        return jax.tree.map(lambda new, old: jnp.where(position < mine, new, old), longer, running)

    return lax.fori_loop(0, count - 1, lap, running)


def own_then_peers(flat, axis, collective_id):
    size = flat.shape[0]
    padded = -(-size // 1024) * 1024
    tiles = jnp.pad(flat, (0, padded - size)).reshape(padded // 128, 128)
    gathered = peer_gather(tiles, axis, "all", collective_id)
    slots = lax.broadcasted_iota(jnp.int32, gathered.shape, 0)
    filled = jnp.where(slots == lax.axis_index(axis), tiles[None], gathered)
    return filled.reshape(gathered.shape[0], padded)[:, :size]


def rounded(values):
    return values.astype(jnp.bfloat16).astype(jnp.float32)


def norm_scale(values):
    return lax.rsqrt(jnp.mean(values * values, axis=-1, keepdims=True) + EPSILON)


def unit_rows(values):
    return values * lax.rsqrt(jnp.sum(values * values, axis=-1, keepdims=True) + EPSILON)


def norm_back(grad_normed, gain_f, x_hat, scales):
    shaped = grad_normed * gain_f
    return scales * (shaped - x_hat * jnp.mean(shaped * x_hat, axis=-1, keepdims=True))


def conv_features(padded, weights, keeping):
    taps_all = weights.shape[0]
    length = keeping.shape[1]
    summed = weights[taps_all - 1] * padded[taps_all - 1 :]
    for offset in range(1, taps_all):
        begin_at = taps_all - 1 - offset
        summed = (
            summed
            + weights[begin_at]
            * padded[begin_at : begin_at + length]
            * keeping[offset - 1][:, None, None]
        )
    active = jax.nn.silu(summed)
    return (unit_rows(active[..., :DK]), unit_rows(active[..., DK : 2 * DK]), active[..., 2 * DK :])


def rate_terms(rate_rows, a_log, dt_bias):
    strength = jax.nn.sigmoid(rate_rows[..., 1])
    log_decay = -jnp.exp(a_log) * jax.nn.softplus(rate_rows[..., 0] + dt_bias)
    return (strength, log_decay)


def gated_norm(core_rows, gate_rows, gain_rows):
    return core_rows * norm_scale(core_rows) * gain_rows * jax.nn.silu(gate_rows)


def swiglu(gate_up):
    return jax.nn.silu(gate_up[:, 0]) * gate_up[:, 1]


def batched_mm(left_mat, right_mat):
    return jnp.einsum("hij,hjk->hik", left_mat, right_mat, precision=FAST_ARITHMETIC)


def compose(earlier, later):
    return (batched_mm(later[0], earlier[0]), batched_mm(later[0], earlier[1]) + later[1])


def unit_lower_inverse(lower_mat):
    size = lower_mat.shape[-1]
    rows = lax.broadcasted_iota(jnp.int32, (size, size), 0)
    cols = lax.broadcasted_iota(jnp.int32, (size, size), 1)
    eye = (rows == cols).astype(lower_mat.dtype)
    strict = lower_mat - eye
    inverse = eye
    width = 1
    while width < size:
        within = ((rows // (2 * width)) == (cols // (2 * width))) & (
            (rows // width) != (cols // width)
        )
        off = strict * within.astype(lower_mat.dtype)
        if width == 1:
            inverse = eye - off
        else:
            inverse = inverse - jnp.einsum(
                "...ij,...jk->...ik",
                inverse,
                jnp.einsum("...ij,...jk->...ik", off, inverse, precision=EXACT_ARITHMETIC),
                precision=EXACT_ARITHMETIC,
            )
        width *= 2
    return inverse


def delta_local(query, keys, values, strength, log_decay, resets):
    length, head_count, key_size = keys.shape
    payload_dimension = values.shape[-1]
    number_of_segments = length // GROUP

    def blocked(array):
        shaped = array.reshape((number_of_segments, GROUP, head_count) + array.shape[2:])
        return jnp.moveaxis(shaped, 2, 1)

    stacked = jnp.concatenate(
        [values, jnp.zeros((length, head_count, key_size), jnp.float32)], axis=-1
    )
    query_b = blocked(query * key_size ** (-0.5))
    keys_b = blocked(keys)
    stacked_b = blocked(stacked)
    strength_b = blocked(strength)
    decay_sum = jnp.cumsum(blocked(log_decay), axis=-1)
    pieces = jnp.cumsum(resets.reshape(number_of_segments, GROUP), axis=-1)
    row_ids = lax.broadcasted_iota(jnp.int32, (GROUP, GROUP), 0)
    col_ids = lax.broadcasted_iota(jnp.int32, (GROUP, GROUP), 1)
    joined = pieces[:, :, None] == pieces[:, None, :]
    inside = (joined & (row_ids >= col_ids))[:, None].astype(jnp.float32)
    before = (joined & (row_ids > col_ids))[:, None].astype(jnp.float32)
    spread = decay_sum[..., :, None] - decay_sum[..., None, :]
    decays = jnp.exp(jnp.where(inside > 0, spread, 0.0)) * inside
    from_start = jnp.exp(decay_sum) * (pieces == 0)[:, None, :].astype(jnp.float32)
    to_end = jnp.exp(decay_sum[..., -1:] - decay_sum) * (pieces == pieces[:, -1:])[
        :, None, :
    ].astype(jnp.float32)
    key_dots = jnp.einsum("nhtk,nhjk->nhtj", keys_b, keys_b, precision=FAST_ARITHMETIC)
    lower_mat = (
        jnp.eye(GROUP, dtype=jnp.float32) + key_dots * decays * before * strength_b[..., :, None]
    )

    inverse = unit_lower_inverse(lower_mat)

    def solved(rhs_rows):
        return jnp.einsum("nhtj,nhjw->nhtw", inverse, rhs_rows, precision=FAST_ARITHMETIC)

    value_part = solved(strength_b[..., None] * stacked_b)
    state_part = solved((strength_b * from_start)[..., None] * keys_b)
    query_keys = jnp.einsum("nhtk,nhjk->nhtj", query_b, keys_b, precision=FAST_ARITHMETIC) * decays
    end_keys = to_end[..., None] * keys_b
    initial = jnp.concatenate(
        [
            jnp.zeros((head_count, key_size, payload_dimension), jnp.float32),
            jnp.broadcast_to(
                jnp.eye(key_size, dtype=jnp.float32), (head_count, key_size, key_size)
            ),
        ],
        axis=-1,
    )

    def advance(carried_state, inputs):
        value_rows, state_rows, query_rows, mixing, end_rows, start_decay, block_decay = inputs
        new_values = value_rows - jnp.einsum(
            "htk,hkw->htw", state_rows, carried_state, precision=FAST_ARITHMETIC
        )
        emitted = start_decay[..., None] * jnp.einsum(
            "htk,hkw->htw", query_rows, carried_state, precision=FAST_ARITHMETIC
        ) + jnp.einsum("htj,hjw->htw", mixing, new_values, precision=FAST_ARITHMETIC)
        carried_state = block_decay[:, None, None] * carried_state + jnp.einsum(
            "hjk,hjw->hkw", end_rows, new_values, precision=FAST_ARITHMETIC
        )
        return (carried_state, emitted)

    final_state, emitted_all = lax.scan(
        advance,
        initial,
        (value_part, state_part, query_b, query_keys, end_keys, from_start, from_start[..., -1]),
        unroll=True,
    )
    emitted_all = jnp.moveaxis(emitted_all, 1, 2).reshape(
        length, head_count, payload_dimension + key_size
    )
    return (
        emitted_all[..., :payload_dimension],
        emitted_all[..., payload_dimension:],
        final_state[..., :payload_dimension],
        final_state[..., payload_dimension:],
    )


def shards(
    tokens,
    seg_ids,
    norm1_gain,
    w_mix,
    w_rate,
    conv_w,
    a_log,
    dt_bias,
    out_gain,
    w_out,
    norm2_gain,
    w_up,
    w_down,
    cotangent,
):
    length = tokens.shape[0]
    head_count = w_mix.shape[1]
    taps_all = conv_w.shape[0]
    rim_rows = taps_all - 1
    conv_width = conv_w.shape[2]
    tp_index = lax.axis_index("tp")
    tokens_f = tokens.astype(jnp.float32)
    gain_one = norm1_gain.astype(jnp.float32)
    scale_one = norm_scale(tokens_f)
    x_hat_one = tokens_f * scale_one
    normed_one = (x_hat_one * gain_one).astype(jnp.bfloat16)
    mixed = jnp.einsum("td,dhc->thc", normed_one, w_mix, preferred_element_type=jnp.float32)
    rate_rows = jnp.einsum("td,dhc->thc", normed_one, w_rate, preferred_element_type=jnp.float32)
    conv_rows = mixed[..., :conv_width].astype(jnp.bfloat16)
    gate_rows = mixed[..., conv_width:]
    tail_rows, tail_ids = shifted(
        (conv_rows[length - rim_rows :], seg_ids[length - rim_rows :].astype(jnp.bfloat16)),
        "seq",
        1,
    )
    own_ids = seg_ids.astype(jnp.float32)
    padded_ids = jnp.concatenate([tail_ids.astype(jnp.float32), own_ids])
    keeping = jnp.stack(
        [
            (padded_ids[rim_rows - offset : rim_rows - offset + length] == own_ids).astype(
                jnp.float32
            )
            for offset in range(1, taps_all)
        ]
    )
    resets = (padded_ids[rim_rows - 1 : rim_rows - 1 + length] != own_ids).astype(jnp.float32)
    padded = jnp.concatenate([tail_rows, conv_rows]).astype(jnp.float32)
    features, conv_pull = jax.vjp(
        lambda padded_rows, weights: conv_features(padded_rows, weights, keeping),
        padded,
        conv_w.astype(jnp.float32),
    )
    query = rounded(features[0])
    keys = rounded(features[1])
    values = rounded(features[2])
    (strength, log_decay), rate_pull = jax.vjp(rate_terms, rate_rows, a_log, dt_bias)
    (local_output, probe_destinations, base_state, transfer), delta_pull = jax.vjp(
        lambda q, k, v, b, g: delta_local(q, k, v, b, g, resets),
        query,
        keys,
        values,
        strength,
        log_decay,
    )
    zero_state = jnp.zeros_like(base_state)
    identity_mats = jnp.broadcast_to(jnp.eye(transfer.shape[1], dtype=jnp.float32), transfer.shape)
    entering_memory_matrix = carried_in(
        (transfer, base_state), "seq", compose, (identity_mats, zero_state)
    )[1]
    core_output = local_output + jnp.einsum(
        "vkq,kqp->vkp", probe_destinations, entering_memory_matrix, precision=FAST_ARITHMETIC
    )
    normed_out_f, gate_pull = jax.vjp(
        gated_norm, core_output, gate_rows, out_gain.astype(jnp.float32)
    )
    normed_out = normed_out_f.astype(jnp.bfloat16)
    mixer_part = jnp.einsum("thv,dhv->td", normed_out, w_out, preferred_element_type=jnp.float32)
    gain_two = norm2_gain.astype(jnp.float32)
    residual = tokens_f + lax.psum(mixer_part.astype(jnp.bfloat16), "tp").astype(jnp.float32)
    scale_two = norm_scale(residual)
    x_hat_two = residual * scale_two
    normed_two = (x_hat_two * gain_two).astype(jnp.bfloat16)
    gate_up = jnp.einsum("td,dcf->tcf", normed_two, w_up, preferred_element_type=jnp.float32)
    hidden_f, hidden_pull = jax.vjp(swiglu, gate_up)
    hidden = hidden_f.astype(jnp.bfloat16)
    ffn_part = jnp.einsum("tf,df->td", hidden, w_down, preferred_element_type=jnp.float32)
    grad_down = jnp.einsum("tf,td->df", hidden, cotangent, preferred_element_type=jnp.float32)
    grad_hidden = jnp.einsum("td,df->tf", cotangent, w_down, preferred_element_type=jnp.float32)
    grad_gate_up = hidden_pull(grad_hidden)[0].astype(jnp.bfloat16)
    grad_up = jnp.einsum(
        "td,tcf->dcf", normed_two, grad_gate_up, preferred_element_type=jnp.float32
    )
    ffn_in_part = jnp.einsum("tcf,dcf->td", grad_gate_up, w_up, preferred_element_type=jnp.float32)
    ffn_in = lax.psum(ffn_in_part.astype(jnp.bfloat16), "tp").astype(jnp.float32)
    gain_two_grad = jnp.sum(ffn_in_part * x_hat_two, axis=0)
    grad_residual = cotangent.astype(jnp.float32) + norm_back(
        ffn_in, gain_two, x_hat_two, scale_two
    )
    grad_mixer = grad_residual.astype(jnp.bfloat16)
    grad_w_out = jnp.einsum(
        "td,thv->dhv", grad_mixer, normed_out, preferred_element_type=jnp.float32
    )
    grad_normed_out = jnp.einsum(
        "td,dhv->thv", grad_mixer, w_out, preferred_element_type=jnp.float32
    )
    core_output_grad, grad_gate_rows, out_gain_grad = gate_pull(grad_normed_out)
    own_state_gradient = jnp.einsum(
        "eyc,eyn->ycn", probe_destinations, core_output_grad, precision=FAST_ARITHMETIC
    )
    transfer_t = jnp.swapaxes(transfer, 1, 2)
    state_gradient = carried_in_2(
        (transfer_t, own_state_gradient), "seq", compose, (identity_mats, zero_state)
    )[1]
    branch_derivatives = jnp.einsum(
        "xao,aeo->xae", core_output_grad, entering_memory_matrix, precision=FAST_ARITHMETIC
    )
    transfer_gradient = jnp.einsum(
        "zne,zye->zny", state_gradient, entering_memory_matrix, precision=FAST_ARITHMETIC
    )
    ffn_send, early_send, state_gradient = lax.optimization_barrier(
        (
            ffn_part.astype(jnp.bfloat16),
            tuple(part.astype(jnp.bfloat16) for part in (grad_w_out, grad_up, grad_down)),
            state_gradient,
        )
    )
    ffn_sum = lax.psum(ffn_send, "tp")
    early_sums = tuple(
        lax.psum_scatter(part, "seq", scatter_dimension=0, tiled=True) for part in early_send
    )
    delta_grads = delta_pull(
        (core_output_grad, branch_derivatives, state_gradient, transfer_gradient)
    )
    ffn_sum, early_sums, delta_grads = lax.optimization_barrier(
        (ffn_sum, early_sums, delta_grads)
    )
    grad_query, grad_keys, grad_values, grad_strength, grad_decay = delta_grads
    layer_out = (residual + ffn_sum.astype(jnp.float32)).astype(jnp.bfloat16)
    grad_rate_rows, a_log_grad, dt_bias_grad = rate_pull((grad_strength, grad_decay))
    grad_padded, conv_grad = conv_pull((grad_query, grad_keys, grad_values))
    back_rows = shifted(grad_padded[:rim_rows], "seq", -1)
    grad_conv_rows = grad_padded[rim_rows:] + jnp.concatenate(
        [jnp.zeros((length - rim_rows,) + back_rows.shape[1:], jnp.float32), back_rows]
    )
    grad_mixed = jnp.concatenate([grad_conv_rows, grad_gate_rows], axis=-1).astype(jnp.bfloat16)
    grad_rates = grad_rate_rows.astype(jnp.bfloat16)
    grad_mix = jnp.einsum("td,thc->dhc", normed_one, grad_mixed, preferred_element_type=jnp.float32)
    grad_rate = jnp.einsum(
        "td,thc->dhc", normed_one, grad_rates, preferred_element_type=jnp.float32
    )
    mixer_in_part = jnp.einsum(
        "thc,dhc->td", grad_mixed, w_mix, preferred_element_type=jnp.float32
    ) + jnp.einsum("thc,dhc->td", grad_rates, w_rate, preferred_element_type=jnp.float32)
    mixer_in = lax.psum(mixer_in_part.astype(jnp.bfloat16), "tp").astype(jnp.float32)
    gain_one_grad = jnp.sum(mixer_in_part * x_hat_one, axis=0)
    grad_tokens = (grad_residual + norm_back(mixer_in, gain_one, x_hat_one, scale_one)).astype(
        jnp.bfloat16
    )
    seq_index = lax.axis_index("seq")
    tp_count = lax.axis_size("tp")
    seq_parts = (gain_one_grad, gain_two_grad, out_gain_grad, conv_grad, a_log_grad, dt_bias_grad)
    seq_summed = own_then_peers(
        jnp.concatenate([part.reshape(-1) for part in seq_parts] + [grad_rate.reshape(-1)]),
        "seq",
        3,
    )
    seq_summed = jnp.sum(seq_summed, axis=0)
    tp_size = sum(part.size for part in seq_parts)
    rate_rows = grad_rate.shape[0] // lax.axis_size("seq")
    rate_sum = lax.dynamic_slice_in_dim(
        seq_summed[tp_size:].reshape(grad_rate.shape), seq_index * rate_rows, rate_rows, 0
    )
    by_tp = own_then_peers(seq_summed[:tp_size], "tp", 4)
    small_sums = []
    start_at = 0
    for part in seq_parts:
        piece = by_tp[:, start_at : start_at + part.size]
        start_at += part.size
        if part.ndim == 1 and part.shape[0] != head_count:
            small_sums.append(jnp.sum(piece, axis=0))
        elif part.ndim == 1:
            small_sums.append(piece.reshape(tp_count * head_count))
        else:
            small_sums.append(
                jnp.moveaxis(piece.reshape((tp_count,) + part.shape), 0, 1).reshape(
                    (taps_all, tp_count * head_count, conv_width)
                )
            )
    weight_sums = (
        lax.psum_scatter(
            grad_mix.astype(jnp.bfloat16), "seq", scatter_dimension=0, tiled=True
        ).astype(jnp.float32),
        rate_sum,
        early_sums[0].astype(jnp.float32),
        early_sums[1].astype(jnp.float32),
        early_sums[2].astype(jnp.float32),
    )
    return (
        layer_out,
        grad_tokens,
        small_sums[0],
        weight_sums[0],
        weight_sums[1],
        small_sums[3],
        small_sums[4],
        small_sums[5],
        small_sums[2],
        weight_sums[2],
        small_sums[1],
        weight_sums[3],
        weight_sums[4],
    )


def solution(mesh):
    in_specs = (
        P("seq", None),
        P("seq"),
        P(),
        P(None, "tp", None),
        P(None, "tp", None),
        P(None, "tp", None),
        P("tp"),
        P("tp"),
        P(),
        P(None, "tp", None),
        P(),
        P(None, None, "tp"),
        P(None, "tp"),
        P("seq", None),
    )
    out_specs = (
        P("seq", None),
        P("seq", None),
        P(),
        P("seq", "tp", None),
        P("seq", "tp", None),
        P(),
        P(),
        P(),
        P(),
        P("seq", "tp", None),
        P(),
        P("seq", None, "tp"),
        P("seq", "tp"),
    )
    return jax.shard_map(shards, mesh=mesh, in_specs=in_specs, out_specs=out_specs, check_vma=False)
```

```python
import functools

import jax
import jax.numpy as jnp
from jax import lax
from jax.experimental import pallas as pl
from jax.experimental.pallas import tpu as pltpu
from jax.sharding import PartitionSpec as P

MESH_IDS = pl.DeviceIdType.MESH

DK = 128
GROUP = 64


EPSILON = 1e-06
EXACT_ARITHMETIC = lax.Precision.HIGHEST
FAST_ARITHMETIC = lax.Precision.HIGH


def shifted(block, axis, distance):
    devices = range(lax.axis_size(axis))
    route = [(i - distance, i) for i in devices if i - distance in devices]
    return lax.ppermute(block, axis, route)


def peer_gather_kernel(axis, count, mode, x_ref, out_ref, send_sem, recv_sem):
    me = lax.axis_index(axis)
    barrier = pltpu.get_barrier_semaphore()
    for step in range(1, count):
        pl.semaphore_signal(
            barrier, inc=1, device_id={axis: lax.rem(me + step, count)}, device_id_type=MESH_IDS
        )
    pl.semaphore_wait(barrier, count - 1)

    def link(step, source, target):
        return pltpu.make_async_remote_copy(
            src_ref=x_ref,
            dst_ref=out_ref.at[source],
            send_sem=send_sem.at[step],
            recv_sem=recv_sem.at[step],
            device_id={axis: target},
            device_id_type=MESH_IDS,
        )

    def target_of(step):
        if mode == "up":
            return me + step, me + step < count
        if mode == "down":
            return me - step, me - step >= 0
        return lax.rem(me + step, count), me >= 0

    def source_of(step):
        if mode == "up":
            return me - step, me - step >= 0
        if mode == "down":
            return me + step, me + step < count
        return lax.rem(me + count - step, count), me >= 0

    for step in range(1, count):
        target, sending = target_of(step)

        @pl.when(sending)
        def _():
            link(step, me, target).start()

    for step in range(1, count):
        target, sending = target_of(step)
        source, receiving = source_of(step)

        @pl.when(sending)
        def _():
            link(step, me, target).wait_send()

        @pl.when(receiving)
        def _():
            link(step, source, source).wait_recv()


def peer_gather(x, axis, mode, collective_id):
    count = lax.axis_size(axis)
    return pl.pallas_call(
        functools.partial(peer_gather_kernel, axis, count, mode),
        out_shape=jax.ShapeDtypeStruct((count,) + x.shape, x.dtype),
        in_specs=[pl.BlockSpec(memory_space=pl.ANY)],
        out_specs=pl.BlockSpec(memory_space=pl.ANY),
        scratch_shapes=[pltpu.SemaphoreType.DMA((count,)), pltpu.SemaphoreType.DMA((count,))],
        compiler_params=pltpu.CompilerParams(collective_id=collective_id, has_side_effects=True),
    )(x)


def joined_gather(value, axis, mode, collective_id, kind):
    widths = [part.shape[-1] for part in value]
    packed = jnp.concatenate([part.astype(kind) for part in value], axis=-1)
    gathered = peer_gather(packed, axis, mode, collective_id)
    pieces = []
    start_at = 0
    for width in widths:
        pieces.append(gathered[..., start_at : start_at + width])
        start_at += width
    return tuple(pieces)


def carried_in(value, axis, join, neutral):
    place = lax.axis_index(axis)
    gathered = joined_gather(value, axis, "up", 1, jnp.bfloat16)
    state = jax.tree.map(lambda a, e: jnp.zeros_like(a) + jnp.asarray(e, a.dtype), value, neutral)

    def one(lap, state):
        return join(
            state,
            jax.tree.map(
                lambda a, own: lax.dynamic_index_in_dim(a, lap, 0, False).astype(own.dtype),
                gathered,
                value,
            ),
        )

    return lax.fori_loop(0, place, one, state)


def carried_in_2(value, axis, join, neutral):
    count, mine = (lax.axis_size(axis), lax.axis_index(axis))
    pieces = jax.tree.map(
        lambda part: lax.all_gather(part.astype(jnp.bfloat16), axis).astype(part.dtype), value
    )
    pieces = jax.tree.map(lambda part: part[::-1], pieces)
    mine = count - 1 - mine
    running = jax.tree.map(
        lambda part, zero: jnp.full_like(part, 0) + jnp.asarray(zero, part.dtype), value, neutral
    )

    def lap(position, running):
        longer = join(running, jax.tree.map(lambda part: part[position], pieces))
        return jax.tree.map(lambda new, old: jnp.where(position < mine, new, old), longer, running)

    return lax.fori_loop(0, count - 1, lap, running)


def own_then_peers(flat, axis, collective_id):
    size = flat.shape[0]
    padded = -(-size // 1024) * 1024
    tiles = jnp.pad(flat, (0, padded - size)).reshape(padded // 128, 128)
    gathered = peer_gather(tiles, axis, "all", collective_id)
    slots = lax.broadcasted_iota(jnp.int32, gathered.shape, 0)
    filled = jnp.where(slots == lax.axis_index(axis), tiles[None], gathered)
    return filled.reshape(gathered.shape[0], padded)[:, :size]


def rounded(values):
    return values.astype(jnp.bfloat16).astype(jnp.float32)


def norm_scale(values):
    return lax.rsqrt(jnp.mean(values * values, axis=-1, keepdims=True) + EPSILON)


def unit_rows(values):
    return values * lax.rsqrt(jnp.sum(values * values, axis=-1, keepdims=True) + EPSILON)


def norm_back(grad_normed, gain_f, x_hat, scales):
    shaped = grad_normed * gain_f
    return scales * (shaped - x_hat * jnp.mean(shaped * x_hat, axis=-1, keepdims=True))


def conv_features(padded, weights, keeping):
    taps_all = weights.shape[0]
    length = keeping.shape[1]
    summed = weights[taps_all - 1] * padded[taps_all - 1 :]
    for offset in range(1, taps_all):
        begin_at = taps_all - 1 - offset
        summed = (
            summed
            + weights[begin_at]
            * padded[begin_at : begin_at + length]
            * keeping[offset - 1][:, None, None]
        )
    active = jax.nn.silu(summed)
    return (unit_rows(active[..., :DK]), unit_rows(active[..., DK : 2 * DK]), active[..., 2 * DK :])


def rate_terms(rate_rows, a_log, dt_bias):
    strength = jax.nn.sigmoid(rate_rows[..., 1])
    log_decay = -jnp.exp(a_log) * jax.nn.softplus(rate_rows[..., 0] + dt_bias)
    return (strength, log_decay)


def gated_norm(core_rows, gate_rows, gain_rows):
    return core_rows * norm_scale(core_rows) * gain_rows * jax.nn.silu(gate_rows)


def swiglu(gate_up):
    return jax.nn.silu(gate_up[:, 0]) * gate_up[:, 1]


def batched_mm(left_mat, right_mat):
    return jnp.einsum("hij,hjk->hik", left_mat, right_mat, precision=FAST_ARITHMETIC)


def compose(earlier, later):
    return (batched_mm(later[0], earlier[0]), batched_mm(later[0], earlier[1]) + later[1])


def unit_lower_inverse(lower_mat):
    size = lower_mat.shape[-1]
    rows = lax.broadcasted_iota(jnp.int32, (size, size), 0)
    cols = lax.broadcasted_iota(jnp.int32, (size, size), 1)
    eye = (rows == cols).astype(lower_mat.dtype)
    strict = lower_mat - eye
    inverse = eye
    width = 1
    while width < size:
        within = ((rows // (2 * width)) == (cols // (2 * width))) & (
            (rows // width) != (cols // width)
        )
        off = strict * within.astype(lower_mat.dtype)
        if width == 1:
            inverse = eye - off
        else:
            inverse = inverse - jnp.einsum(
                "...ij,...jk->...ik",
                inverse,
                jnp.einsum("...ij,...jk->...ik", off, inverse, precision=EXACT_ARITHMETIC),
                precision=EXACT_ARITHMETIC,
            )
        width *= 2
    return inverse


def delta_local(query, keys, values, strength, log_decay, resets):
    length, head_count, key_size = keys.shape
    payload_dimension = values.shape[-1]
    number_of_segments = length // GROUP

    def blocked(array):
        shaped = array.reshape((number_of_segments, GROUP, head_count) + array.shape[2:])
        return jnp.moveaxis(shaped, 2, 1)

    stacked = jnp.concatenate(
        [values, jnp.zeros((length, head_count, key_size), jnp.float32)], axis=-1
    )
    query_b = blocked(query * key_size ** (-0.5))
    keys_b = blocked(keys)
    stacked_b = blocked(stacked)
    strength_b = blocked(strength)
    decay_sum = jnp.cumsum(blocked(log_decay), axis=-1)
    pieces = jnp.cumsum(resets.reshape(number_of_segments, GROUP), axis=-1)
    row_ids = lax.broadcasted_iota(jnp.int32, (GROUP, GROUP), 0)
    col_ids = lax.broadcasted_iota(jnp.int32, (GROUP, GROUP), 1)
    joined = pieces[:, :, None] == pieces[:, None, :]
    inside = (joined & (row_ids >= col_ids))[:, None].astype(jnp.float32)
    before = (joined & (row_ids > col_ids))[:, None].astype(jnp.float32)
    spread = decay_sum[..., :, None] - decay_sum[..., None, :]
    decays = jnp.exp(jnp.where(inside > 0, spread, 0.0)) * inside
    from_start = jnp.exp(decay_sum) * (pieces == 0)[:, None, :].astype(jnp.float32)
    to_end = jnp.exp(decay_sum[..., -1:] - decay_sum) * (pieces == pieces[:, -1:])[
        :, None, :
    ].astype(jnp.float32)
    key_dots = jnp.einsum("nhtk,nhjk->nhtj", keys_b, keys_b, precision=FAST_ARITHMETIC)
    lower_mat = (
        jnp.eye(GROUP, dtype=jnp.float32) + key_dots * decays * before * strength_b[..., :, None]
    )

    inverse = unit_lower_inverse(lower_mat)

    def solved(rhs_rows):
        return jnp.einsum("nhtj,nhjw->nhtw", inverse, rhs_rows, precision=FAST_ARITHMETIC)

    value_part = solved(strength_b[..., None] * stacked_b)
    state_part = solved((strength_b * from_start)[..., None] * keys_b)
    query_keys = jnp.einsum("nhtk,nhjk->nhtj", query_b, keys_b, precision=FAST_ARITHMETIC) * decays
    end_keys = to_end[..., None] * keys_b
    initial = jnp.concatenate(
        [
            jnp.zeros((head_count, key_size, payload_dimension), jnp.float32),
            jnp.broadcast_to(
                jnp.eye(key_size, dtype=jnp.float32), (head_count, key_size, key_size)
            ),
        ],
        axis=-1,
    )

    def advance(carried_state, inputs):
        value_rows, state_rows, query_rows, mixing, end_rows, start_decay, block_decay = inputs
        new_values = value_rows - jnp.einsum(
            "htk,hkw->htw", state_rows, carried_state, precision=FAST_ARITHMETIC
        )
        emitted = start_decay[..., None] * jnp.einsum(
            "htk,hkw->htw", query_rows, carried_state, precision=FAST_ARITHMETIC
        ) + jnp.einsum("htj,hjw->htw", mixing, new_values, precision=FAST_ARITHMETIC)
        carried_state = block_decay[:, None, None] * carried_state + jnp.einsum(
            "hjk,hjw->hkw", end_rows, new_values, precision=FAST_ARITHMETIC
        )
        return (carried_state, emitted)

    final_state, emitted_all = lax.scan(
        advance,
        initial,
        (value_part, state_part, query_b, query_keys, end_keys, from_start, from_start[..., -1]),
        unroll=True,
    )
    emitted_all = jnp.moveaxis(emitted_all, 1, 2).reshape(
        length, head_count, payload_dimension + key_size
    )
    return (
        emitted_all[..., :payload_dimension],
        emitted_all[..., payload_dimension:],
        final_state[..., :payload_dimension],
        final_state[..., payload_dimension:],
    )


def shards(
    tokens,
    seg_ids,
    norm1_gain,
    w_mix,
    w_rate,
    conv_w,
    a_log,
    dt_bias,
    out_gain,
    w_out,
    norm2_gain,
    w_up,
    w_down,
    cotangent,
):
    length = tokens.shape[0]
    head_count = w_mix.shape[1]
    taps_all = conv_w.shape[0]
    rim_rows = taps_all - 1
    conv_width = conv_w.shape[2]
    tp_index = lax.axis_index("tp")
    tokens_f = tokens.astype(jnp.float32)
    gain_one = norm1_gain.astype(jnp.float32)
    scale_one = norm_scale(tokens_f)
    x_hat_one = tokens_f * scale_one
    normed_one = (x_hat_one * gain_one).astype(jnp.bfloat16)
    mixed = jnp.einsum("td,dhc->thc", normed_one, w_mix, preferred_element_type=jnp.float32)
    rate_rows = jnp.einsum("td,dhc->thc", normed_one, w_rate, preferred_element_type=jnp.float32)
    conv_rows = mixed[..., :conv_width].astype(jnp.bfloat16)
    gate_rows = mixed[..., conv_width:]
    tail_rows, tail_ids = shifted(
        (conv_rows[length - rim_rows :], seg_ids[length - rim_rows :].astype(jnp.bfloat16)),
        "seq",
        1,
    )
    own_ids = seg_ids.astype(jnp.float32)
    padded_ids = jnp.concatenate([tail_ids.astype(jnp.float32), own_ids])
    keeping = jnp.stack(
        [
            (padded_ids[rim_rows - offset : rim_rows - offset + length] == own_ids).astype(
                jnp.float32
            )
            for offset in range(1, taps_all)
        ]
    )
    resets = (padded_ids[rim_rows - 1 : rim_rows - 1 + length] != own_ids).astype(jnp.float32)
    padded = jnp.concatenate([tail_rows, conv_rows]).astype(jnp.float32)
    features, conv_pull = jax.vjp(
        lambda padded_rows, weights: conv_features(padded_rows, weights, keeping),
        padded,
        conv_w.astype(jnp.float32),
    )
    query = rounded(features[0])
    keys = rounded(features[1])
    values = rounded(features[2])
    (strength, log_decay), rate_pull = jax.vjp(rate_terms, rate_rows, a_log, dt_bias)
    (local_output, probe_destinations, base_state, transfer), delta_pull = jax.vjp(
        lambda q, k, v, b, g: delta_local(q, k, v, b, g, resets),
        query,
        keys,
        values,
        strength,
        log_decay,
    )
    zero_state = jnp.zeros_like(base_state)
    identity_mats = jnp.broadcast_to(jnp.eye(transfer.shape[1], dtype=jnp.float32), transfer.shape)
    entering_memory_matrix = carried_in(
        (transfer, base_state), "seq", compose, (identity_mats, zero_state)
    )[1]
    core_output = local_output + jnp.einsum(
        "vkq,kqp->vkp", probe_destinations, entering_memory_matrix, precision=FAST_ARITHMETIC
    )
    normed_out_f, gate_pull = jax.vjp(
        gated_norm, core_output, gate_rows, out_gain.astype(jnp.float32)
    )
    normed_out = normed_out_f.astype(jnp.bfloat16)
    mixer_part = jnp.einsum("thv,dhv->td", normed_out, w_out, preferred_element_type=jnp.float32)
    gain_two = norm2_gain.astype(jnp.float32)
    residual = tokens_f + lax.psum(mixer_part.astype(jnp.bfloat16), "tp").astype(jnp.float32)
    scale_two = norm_scale(residual)
    x_hat_two = residual * scale_two
    normed_two = (x_hat_two * gain_two).astype(jnp.bfloat16)
    gate_up = jnp.einsum("td,dcf->tcf", normed_two, w_up, preferred_element_type=jnp.float32)
    hidden_f, hidden_pull = jax.vjp(swiglu, gate_up)
    hidden = hidden_f.astype(jnp.bfloat16)
    ffn_part = jnp.einsum("tf,df->td", hidden, w_down, preferred_element_type=jnp.float32)
    grad_down = jnp.einsum("tf,td->df", hidden, cotangent, preferred_element_type=jnp.float32)
    grad_hidden = jnp.einsum("td,df->tf", cotangent, w_down, preferred_element_type=jnp.float32)
    grad_gate_up = hidden_pull(grad_hidden)[0].astype(jnp.bfloat16)
    grad_up = jnp.einsum(
        "td,tcf->dcf", normed_two, grad_gate_up, preferred_element_type=jnp.float32
    )
    ffn_in_part = jnp.einsum("tcf,dcf->td", grad_gate_up, w_up, preferred_element_type=jnp.float32)
    ffn_in = lax.psum(ffn_in_part.astype(jnp.bfloat16), "tp").astype(jnp.float32)
    gain_two_grad = jnp.sum(ffn_in_part * x_hat_two, axis=0)
    grad_residual = cotangent.astype(jnp.float32) + norm_back(
        ffn_in, gain_two, x_hat_two, scale_two
    )
    grad_mixer = grad_residual.astype(jnp.bfloat16)
    grad_w_out = jnp.einsum(
        "td,thv->dhv", grad_mixer, normed_out, preferred_element_type=jnp.float32
    )
    grad_normed_out = jnp.einsum(
        "td,dhv->thv", grad_mixer, w_out, preferred_element_type=jnp.float32
    )
    core_output_grad, grad_gate_rows, out_gain_grad = gate_pull(grad_normed_out)
    own_state_gradient = jnp.einsum(
        "eyc,eyn->ycn", probe_destinations, core_output_grad, precision=FAST_ARITHMETIC
    )
    transfer_t = jnp.swapaxes(transfer, 1, 2)
    state_gradient = carried_in_2(
        (transfer_t, own_state_gradient), "seq", compose, (identity_mats, zero_state)
    )[1]
    branch_derivatives = jnp.einsum(
        "xao,aeo->xae", core_output_grad, entering_memory_matrix, precision=FAST_ARITHMETIC
    )
    transfer_gradient = jnp.einsum(
        "zne,zye->zny", state_gradient, entering_memory_matrix, precision=FAST_ARITHMETIC
    )
    ffn_send, early_send, state_gradient = lax.optimization_barrier(
        (
            ffn_part.astype(jnp.bfloat16),
            tuple(part.astype(jnp.bfloat16) for part in (grad_w_out, grad_up, grad_down)),
            state_gradient,
        )
    )
    ffn_sum = lax.psum(ffn_send, "tp")
    early_sums = tuple(
        lax.psum_scatter(part, "seq", scatter_dimension=0, tiled=True) for part in early_send
    )
    delta_grads = delta_pull(
        (core_output_grad, branch_derivatives, state_gradient, transfer_gradient)
    )
    grad_query, grad_keys, grad_values, grad_strength, grad_decay = delta_grads
    grad_rate_rows, a_log_grad, dt_bias_grad = rate_pull((grad_strength, grad_decay))
    grad_padded, conv_grad = conv_pull((grad_query, grad_keys, grad_values))
    back_rows = shifted(grad_padded[:rim_rows], "seq", -1)
    grad_conv_rows = grad_padded[rim_rows:] + jnp.concatenate(
        [jnp.zeros((length - rim_rows,) + back_rows.shape[1:], jnp.float32), back_rows]
    )
    grad_mixed = jnp.concatenate([grad_conv_rows, grad_gate_rows], axis=-1).astype(jnp.bfloat16)
    ffn_sum, early_sums, grad_mixed = lax.optimization_barrier((ffn_sum, early_sums, grad_mixed))
    layer_out = (residual + ffn_sum.astype(jnp.float32)).astype(jnp.bfloat16)
    grad_rates = grad_rate_rows.astype(jnp.bfloat16)
    grad_mix = jnp.einsum("td,thc->dhc", normed_one, grad_mixed, preferred_element_type=jnp.float32)
    grad_rate = jnp.einsum(
        "td,thc->dhc", normed_one, grad_rates, preferred_element_type=jnp.float32
    )
    mixer_in_part = jnp.einsum(
        "thc,dhc->td", grad_mixed, w_mix, preferred_element_type=jnp.float32
    ) + jnp.einsum("thc,dhc->td", grad_rates, w_rate, preferred_element_type=jnp.float32)
    mixer_in = lax.psum(mixer_in_part.astype(jnp.bfloat16), "tp").astype(jnp.float32)
    gain_one_grad = jnp.sum(mixer_in_part * x_hat_one, axis=0)
    grad_tokens = (grad_residual + norm_back(mixer_in, gain_one, x_hat_one, scale_one)).astype(
        jnp.bfloat16
    )
    seq_index = lax.axis_index("seq")
    tp_count = lax.axis_size("tp")
    seq_parts = (gain_one_grad, gain_two_grad, out_gain_grad, conv_grad, a_log_grad, dt_bias_grad)
    seq_summed = own_then_peers(
        jnp.concatenate([part.reshape(-1) for part in seq_parts] + [grad_rate.reshape(-1)]),
        "seq",
        3,
    )
    seq_summed = jnp.sum(seq_summed, axis=0)
    tp_size = sum(part.size for part in seq_parts)
    rate_rows = grad_rate.shape[0] // lax.axis_size("seq")
    rate_sum = lax.dynamic_slice_in_dim(
        seq_summed[tp_size:].reshape(grad_rate.shape), seq_index * rate_rows, rate_rows, 0
    )
    by_tp = own_then_peers(seq_summed[:tp_size], "tp", 4)
    small_sums = []
    start_at = 0
    for part in seq_parts:
        piece = by_tp[:, start_at : start_at + part.size]
        start_at += part.size
        if part.ndim == 1 and part.shape[0] != head_count:
            small_sums.append(jnp.sum(piece, axis=0))
        elif part.ndim == 1:
            small_sums.append(piece.reshape(tp_count * head_count))
        else:
            small_sums.append(
                jnp.moveaxis(piece.reshape((tp_count,) + part.shape), 0, 1).reshape(
                    (taps_all, tp_count * head_count, conv_width)
                )
            )
    weight_sums = (
        lax.psum_scatter(
            grad_mix.astype(jnp.bfloat16), "seq", scatter_dimension=0, tiled=True
        ).astype(jnp.float32),
        rate_sum,
        early_sums[0].astype(jnp.float32),
        early_sums[1].astype(jnp.float32),
        early_sums[2].astype(jnp.float32),
    )
    return (
        layer_out,
        grad_tokens,
        small_sums[0],
        weight_sums[0],
        weight_sums[1],
        small_sums[3],
        small_sums[4],
        small_sums[5],
        small_sums[2],
        weight_sums[2],
        small_sums[1],
        weight_sums[3],
        weight_sums[4],
    )


def solution(mesh):
    in_specs = (
        P("seq", None),
        P("seq"),
        P(),
        P(None, "tp", None),
        P(None, "tp", None),
        P(None, "tp", None),
        P("tp"),
        P("tp"),
        P(),
        P(None, "tp", None),
        P(),
        P(None, None, "tp"),
        P(None, "tp"),
        P("seq", None),
    )
    out_specs = (
        P("seq", None),
        P("seq", None),
        P(),
        P("seq", "tp", None),
        P("seq", "tp", None),
        P(),
        P(),
        P(),
        P(),
        P("seq", "tp", None),
        P(),
        P("seq", None, "tp"),
        P("seq", "tp"),
    )
    return jax.shard_map(shards, mesh=mesh, in_specs=in_specs, out_specs=out_specs, check_vma=False)
```

```python
import functools

import jax
import jax.numpy as jnp
from jax import lax
from jax.experimental import pallas as pl
from jax.experimental.pallas import tpu as pltpu
from jax.sharding import PartitionSpec as P

MESH_IDS = pl.DeviceIdType.MESH

DK = 128
GROUP = 64


EPSILON = 1e-06
EXACT_ARITHMETIC = lax.Precision.HIGHEST
FAST_ARITHMETIC = lax.Precision.HIGH


def shifted(block, axis, distance):
    devices = range(lax.axis_size(axis))
    route = [(i - distance, i) for i in devices if i - distance in devices]
    return lax.ppermute(block, axis, route)


def peer_gather_kernel(axis, count, mode, x_ref, out_ref, send_sem, recv_sem):
    me = lax.axis_index(axis)
    barrier = pltpu.get_barrier_semaphore()
    for step in range(1, count):
        pl.semaphore_signal(
            barrier, inc=1, device_id={axis: lax.rem(me + step, count)}, device_id_type=MESH_IDS
        )
    pl.semaphore_wait(barrier, count - 1)

    def link(step, source, target):
        return pltpu.make_async_remote_copy(
            src_ref=x_ref,
            dst_ref=out_ref.at[source],
            send_sem=send_sem.at[step],
            recv_sem=recv_sem.at[step],
            device_id={axis: target},
            device_id_type=MESH_IDS,
        )

    def target_of(step):
        if mode == "up":
            return me + step, me + step < count
        if mode == "down":
            return me - step, me - step >= 0
        return lax.rem(me + step, count), me >= 0

    def source_of(step):
        if mode == "up":
            return me - step, me - step >= 0
        if mode == "down":
            return me + step, me + step < count
        return lax.rem(me + count - step, count), me >= 0

    for step in range(1, count):
        target, sending = target_of(step)

        @pl.when(sending)
        def _():
            link(step, me, target).start()

    for step in range(1, count):
        target, sending = target_of(step)
        source, receiving = source_of(step)

        @pl.when(sending)
        def _():
            link(step, me, target).wait_send()

        @pl.when(receiving)
        def _():
            link(step, source, source).wait_recv()


def peer_gather(x, axis, mode, collective_id):
    count = lax.axis_size(axis)
    return pl.pallas_call(
        functools.partial(peer_gather_kernel, axis, count, mode),
        out_shape=jax.ShapeDtypeStruct((count,) + x.shape, x.dtype),
        in_specs=[pl.BlockSpec(memory_space=pl.ANY)],
        out_specs=pl.BlockSpec(memory_space=pl.ANY),
        scratch_shapes=[pltpu.SemaphoreType.DMA((count,)), pltpu.SemaphoreType.DMA((count,))],
        compiler_params=pltpu.CompilerParams(collective_id=collective_id, has_side_effects=True),
    )(x)


def joined_gather(value, axis, mode, collective_id, kind):
    widths = [part.shape[-1] for part in value]
    packed = jnp.concatenate([part.astype(kind) for part in value], axis=-1)
    gathered = peer_gather(packed, axis, mode, collective_id)
    pieces = []
    start_at = 0
    for width in widths:
        pieces.append(gathered[..., start_at : start_at + width])
        start_at += width
    return tuple(pieces)


def carried_in(value, axis, join, neutral):
    place = lax.axis_index(axis)
    gathered = joined_gather(value, axis, "up", 1, jnp.bfloat16)
    state = jax.tree.map(lambda a, e: jnp.zeros_like(a) + jnp.asarray(e, a.dtype), value, neutral)

    def one(lap, state):
        return join(
            state,
            jax.tree.map(
                lambda a, own: lax.dynamic_index_in_dim(a, lap, 0, False).astype(own.dtype),
                gathered,
                value,
            ),
        )

    return lax.fori_loop(0, place, one, state)


def carried_in_2(value, axis, join, neutral):
    count, mine = (lax.axis_size(axis), lax.axis_index(axis))
    pieces = jax.tree.map(
        lambda part: lax.all_gather(part.astype(jnp.bfloat16), axis).astype(part.dtype), value
    )
    pieces = jax.tree.map(lambda part: part[::-1], pieces)
    mine = count - 1 - mine
    running = jax.tree.map(
        lambda part, zero: jnp.full_like(part, 0) + jnp.asarray(zero, part.dtype), value, neutral
    )

    def lap(position, running):
        longer = join(running, jax.tree.map(lambda part: part[position], pieces))
        return jax.tree.map(lambda new, old: jnp.where(position < mine, new, old), longer, running)

    return lax.fori_loop(0, count - 1, lap, running)


def own_then_peers(flat, axis, collective_id):
    size = flat.shape[0]
    padded = -(-size // 1024) * 1024
    tiles = jnp.pad(flat, (0, padded - size)).reshape(padded // 128, 128)
    gathered = peer_gather(tiles, axis, "all", collective_id)
    slots = lax.broadcasted_iota(jnp.int32, gathered.shape, 0)
    filled = jnp.where(slots == lax.axis_index(axis), tiles[None], gathered)
    return filled.reshape(gathered.shape[0], padded)[:, :size]


def rounded(values):
    return values.astype(jnp.bfloat16).astype(jnp.float32)


def norm_scale(values):
    return lax.rsqrt(jnp.mean(values * values, axis=-1, keepdims=True) + EPSILON)


def unit_rows(values):
    return values * lax.rsqrt(jnp.sum(values * values, axis=-1, keepdims=True) + EPSILON)


def norm_back(grad_normed, gain_f, x_hat, scales):
    shaped = grad_normed * gain_f
    return scales * (shaped - x_hat * jnp.mean(shaped * x_hat, axis=-1, keepdims=True))


def conv_features(padded, weights, keeping):
    taps_all = weights.shape[0]
    length = keeping.shape[1]
    summed = weights[taps_all - 1] * padded[taps_all - 1 :]
    for offset in range(1, taps_all):
        begin_at = taps_all - 1 - offset
        summed = (
            summed
            + weights[begin_at]
            * padded[begin_at : begin_at + length]
            * keeping[offset - 1][:, None, None]
        )
    active = jax.nn.silu(summed)
    return (unit_rows(active[..., :DK]), unit_rows(active[..., DK : 2 * DK]), active[..., 2 * DK :])


def rate_terms(rate_rows, a_log, dt_bias):
    strength = jax.nn.sigmoid(rate_rows[..., 1])
    log_decay = -jnp.exp(a_log) * jax.nn.softplus(rate_rows[..., 0] + dt_bias)
    return (strength, log_decay)


def gated_norm(core_rows, gate_rows, gain_rows):
    return core_rows * norm_scale(core_rows) * gain_rows * jax.nn.silu(gate_rows)


def swiglu(gate_up):
    return jax.nn.silu(gate_up[:, 0]) * gate_up[:, 1]


def batched_mm(left_mat, right_mat):
    return jnp.einsum("hij,hjk->hik", left_mat, right_mat, precision=FAST_ARITHMETIC)


def compose(earlier, later):
    return (batched_mm(later[0], earlier[0]), batched_mm(later[0], earlier[1]) + later[1])


def unit_lower_inverse(lower_mat):
    size = lower_mat.shape[-1]
    rows = lax.broadcasted_iota(jnp.int32, (size, size), 0)
    cols = lax.broadcasted_iota(jnp.int32, (size, size), 1)
    eye = (rows == cols).astype(lower_mat.dtype)
    strict = lower_mat - eye
    inverse = eye
    width = 1
    while width < size:
        within = ((rows // (2 * width)) == (cols // (2 * width))) & (
            (rows // width) != (cols // width)
        )
        off = strict * within.astype(lower_mat.dtype)
        if width == 1:
            inverse = eye - off
        else:
            inverse = inverse - jnp.einsum(
                "...ij,...jk->...ik",
                inverse,
                jnp.einsum("...ij,...jk->...ik", off, inverse, precision=FAST_ARITHMETIC),
                precision=FAST_ARITHMETIC,
            )
        width *= 2
    return inverse


def delta_local(query, keys, values, strength, log_decay, resets):
    length, head_count, key_size = keys.shape
    payload_dimension = values.shape[-1]
    number_of_segments = length // GROUP

    def blocked(array):
        shaped = array.reshape((number_of_segments, GROUP, head_count) + array.shape[2:])
        return jnp.moveaxis(shaped, 2, 1)

    stacked = jnp.concatenate(
        [values, jnp.zeros((length, head_count, key_size), jnp.float32)], axis=-1
    )
    query_b = blocked(query * key_size ** (-0.5))
    keys_b = blocked(keys)
    stacked_b = blocked(stacked)
    strength_b = blocked(strength)
    decay_sum = jnp.cumsum(blocked(log_decay), axis=-1)
    pieces = jnp.cumsum(resets.reshape(number_of_segments, GROUP), axis=-1)
    row_ids = lax.broadcasted_iota(jnp.int32, (GROUP, GROUP), 0)
    col_ids = lax.broadcasted_iota(jnp.int32, (GROUP, GROUP), 1)
    joined = pieces[:, :, None] == pieces[:, None, :]
    inside = (joined & (row_ids >= col_ids))[:, None].astype(jnp.float32)
    before = (joined & (row_ids > col_ids))[:, None].astype(jnp.float32)
    spread = decay_sum[..., :, None] - decay_sum[..., None, :]
    decays = jnp.exp(jnp.where(inside > 0, spread, 0.0)) * inside
    from_start = jnp.exp(decay_sum) * (pieces == 0)[:, None, :].astype(jnp.float32)
    to_end = jnp.exp(decay_sum[..., -1:] - decay_sum) * (pieces == pieces[:, -1:])[
        :, None, :
    ].astype(jnp.float32)
    key_dots = jnp.einsum(
        "nhtk,nhjk->nhtj", keys_b, keys_b, preferred_element_type=jnp.float32
    )
    lower_mat = (
        jnp.eye(GROUP, dtype=jnp.float32) + key_dots * decays * before * strength_b[..., :, None]
    )

    inverse = unit_lower_inverse(lower_mat)

    def solved(rhs_rows):
        return jnp.einsum("nhtj,nhjw->nhtw", inverse, rhs_rows, precision=FAST_ARITHMETIC)

    value_part = solved(strength_b[..., None] * stacked_b)
    state_part = solved((strength_b * from_start)[..., None] * keys_b)
    query_keys = jnp.einsum("nhtk,nhjk->nhtj", query_b, keys_b, precision=FAST_ARITHMETIC) * decays
    end_keys = to_end[..., None] * keys_b
    initial = jnp.concatenate(
        [
            jnp.zeros((head_count, key_size, payload_dimension), jnp.float32),
            jnp.broadcast_to(
                jnp.eye(key_size, dtype=jnp.float32), (head_count, key_size, key_size)
            ),
        ],
        axis=-1,
    )

    def advance(carried_state, inputs):
        value_rows, state_rows, query_rows, mixing, end_rows, start_decay, block_decay = inputs
        new_values = value_rows - jnp.einsum(
            "htk,hkw->htw", state_rows, carried_state, precision=FAST_ARITHMETIC
        )
        emitted = start_decay[..., None] * jnp.einsum(
            "htk,hkw->htw", query_rows, carried_state, precision=FAST_ARITHMETIC
        ) + jnp.einsum("htj,hjw->htw", mixing, new_values, precision=FAST_ARITHMETIC)
        carried_state = block_decay[:, None, None] * carried_state + jnp.einsum(
            "hjk,hjw->hkw", end_rows, new_values, precision=FAST_ARITHMETIC
        )
        return (carried_state, emitted)

    final_state, emitted_all = lax.scan(
        advance,
        initial,
        (value_part, state_part, query_b, query_keys, end_keys, from_start, from_start[..., -1]),
        unroll=True,
    )
    emitted_all = jnp.moveaxis(emitted_all, 1, 2).reshape(
        length, head_count, payload_dimension + key_size
    )
    return (
        emitted_all[..., :payload_dimension],
        emitted_all[..., payload_dimension:],
        final_state[..., :payload_dimension],
        final_state[..., payload_dimension:],
    )


def shards(
    tokens,
    seg_ids,
    norm1_gain,
    w_mix,
    w_rate,
    conv_w,
    a_log,
    dt_bias,
    out_gain,
    w_out,
    norm2_gain,
    w_up,
    w_down,
    cotangent,
):
    length = tokens.shape[0]
    head_count = w_mix.shape[1]
    taps_all = conv_w.shape[0]
    rim_rows = taps_all - 1
    conv_width = conv_w.shape[2]
    tp_index = lax.axis_index("tp")
    tokens_f = tokens.astype(jnp.float32)
    gain_one = norm1_gain.astype(jnp.float32)
    scale_one = norm_scale(tokens_f)
    x_hat_one = tokens_f * scale_one
    normed_one = (x_hat_one * gain_one).astype(jnp.bfloat16)
    mixed = jnp.einsum("td,dhc->thc", normed_one, w_mix, preferred_element_type=jnp.float32)
    rate_rows = jnp.einsum("td,dhc->thc", normed_one, w_rate, preferred_element_type=jnp.float32)
    conv_rows = mixed[..., :conv_width].astype(jnp.bfloat16)
    gate_rows = mixed[..., conv_width:]
    tail_rows, tail_ids = shifted(
        (conv_rows[length - rim_rows :], seg_ids[length - rim_rows :].astype(jnp.bfloat16)),
        "seq",
        1,
    )
    own_ids = seg_ids.astype(jnp.float32)
    padded_ids = jnp.concatenate([tail_ids.astype(jnp.float32), own_ids])
    keeping = jnp.stack(
        [
            (padded_ids[rim_rows - offset : rim_rows - offset + length] == own_ids).astype(
                jnp.float32
            )
            for offset in range(1, taps_all)
        ]
    )
    resets = (padded_ids[rim_rows - 1 : rim_rows - 1 + length] != own_ids).astype(jnp.float32)
    padded = jnp.concatenate([tail_rows, conv_rows]).astype(jnp.float32)
    features, conv_pull = jax.vjp(
        lambda padded_rows, weights: conv_features(padded_rows, weights, keeping),
        padded,
        conv_w.astype(jnp.float32),
    )
    query = rounded(features[0])
    keys = rounded(features[1])
    values = rounded(features[2])
    (strength, log_decay), rate_pull = jax.vjp(rate_terms, rate_rows, a_log, dt_bias)
    (local_output, probe_destinations, base_state, transfer), delta_pull = jax.vjp(
        lambda q, k, v, b, g: delta_local(q, k, v, b, g, resets),
        query,
        keys,
        values,
        strength,
        log_decay,
    )
    zero_state = jnp.zeros_like(base_state)
    identity_mats = jnp.broadcast_to(jnp.eye(transfer.shape[1], dtype=jnp.float32), transfer.shape)
    entering_memory_matrix = carried_in(
        (transfer, base_state), "seq", compose, (identity_mats, zero_state)
    )[1]
    core_output = local_output + jnp.einsum(
        "vkq,kqp->vkp", probe_destinations, entering_memory_matrix, precision=FAST_ARITHMETIC
    )
    normed_out_f, gate_pull = jax.vjp(
        gated_norm, core_output, gate_rows, out_gain.astype(jnp.float32)
    )
    normed_out = normed_out_f.astype(jnp.bfloat16)
    mixer_part = jnp.einsum("thv,dhv->td", normed_out, w_out, preferred_element_type=jnp.float32)
    gain_two = norm2_gain.astype(jnp.float32)
    residual = tokens_f + lax.psum(mixer_part.astype(jnp.bfloat16), "tp").astype(jnp.float32)
    scale_two = norm_scale(residual)
    x_hat_two = residual * scale_two
    normed_two = (x_hat_two * gain_two).astype(jnp.bfloat16)
    gate_up = jnp.einsum("td,dcf->tcf", normed_two, w_up, preferred_element_type=jnp.float32)
    hidden_f, hidden_pull = jax.vjp(swiglu, gate_up)
    hidden = hidden_f.astype(jnp.bfloat16)
    ffn_part = jnp.einsum("tf,df->td", hidden, w_down, preferred_element_type=jnp.float32)
    grad_down = jnp.einsum("tf,td->df", hidden, cotangent, preferred_element_type=jnp.float32)
    grad_hidden = jnp.einsum("td,df->tf", cotangent, w_down, preferred_element_type=jnp.float32)
    grad_gate_up = hidden_pull(grad_hidden)[0].astype(jnp.bfloat16)
    grad_up = jnp.einsum(
        "td,tcf->dcf", normed_two, grad_gate_up, preferred_element_type=jnp.float32
    )
    ffn_in_part = jnp.einsum("tcf,dcf->td", grad_gate_up, w_up, preferred_element_type=jnp.float32)
    ffn_in = lax.psum(ffn_in_part.astype(jnp.bfloat16), "tp").astype(jnp.float32)
    gain_two_grad = jnp.sum(ffn_in_part * x_hat_two, axis=0)
    grad_residual = cotangent.astype(jnp.float32) + norm_back(
        ffn_in, gain_two, x_hat_two, scale_two
    )
    grad_mixer = grad_residual.astype(jnp.bfloat16)
    grad_w_out = jnp.einsum(
        "td,thv->dhv", grad_mixer, normed_out, preferred_element_type=jnp.float32
    )
    grad_normed_out = jnp.einsum(
        "td,dhv->thv", grad_mixer, w_out, preferred_element_type=jnp.float32
    )
    core_output_grad, grad_gate_rows, out_gain_grad = gate_pull(grad_normed_out)
    own_state_gradient = jnp.einsum(
        "eyc,eyn->ycn", probe_destinations, core_output_grad, precision=FAST_ARITHMETIC
    )
    transfer_t = jnp.swapaxes(transfer, 1, 2)
    state_gradient = carried_in_2(
        (transfer_t, own_state_gradient), "seq", compose, (identity_mats, zero_state)
    )[1]
    branch_derivatives = jnp.einsum(
        "xao,aeo->xae", core_output_grad, entering_memory_matrix, precision=FAST_ARITHMETIC
    )
    transfer_gradient = jnp.einsum(
        "zne,zye->zny", state_gradient, entering_memory_matrix, precision=FAST_ARITHMETIC
    )
    ffn_send, early_send, state_gradient = lax.optimization_barrier(
        (
            ffn_part.astype(jnp.bfloat16),
            tuple(part.astype(jnp.bfloat16) for part in (grad_w_out, grad_up, grad_down)),
            state_gradient,
        )
    )
    ffn_sum = lax.psum(ffn_send, "tp")
    early_sums = tuple(
        lax.psum_scatter(part, "seq", scatter_dimension=0, tiled=True) for part in early_send
    )
    delta_grads = delta_pull(
        (core_output_grad, branch_derivatives, state_gradient, transfer_gradient)
    )
    grad_query, grad_keys, grad_values, grad_strength, grad_decay = delta_grads
    grad_rate_rows, a_log_grad, dt_bias_grad = rate_pull((grad_strength, grad_decay))
    grad_padded, conv_grad = conv_pull((grad_query, grad_keys, grad_values))
    back_rows = shifted(grad_padded[:rim_rows], "seq", -1)
    grad_conv_rows = grad_padded[rim_rows:] + jnp.concatenate(
        [jnp.zeros((length - rim_rows,) + back_rows.shape[1:], jnp.float32), back_rows]
    )
    grad_mixed = jnp.concatenate([grad_conv_rows, grad_gate_rows], axis=-1).astype(jnp.bfloat16)
    ffn_sum, early_sums, grad_mixed = lax.optimization_barrier((ffn_sum, early_sums, grad_mixed))
    layer_out = (residual + ffn_sum.astype(jnp.float32)).astype(jnp.bfloat16)
    grad_rates = grad_rate_rows.astype(jnp.bfloat16)
    grad_mix = jnp.einsum("td,thc->dhc", normed_one, grad_mixed, preferred_element_type=jnp.float32)
    grad_rate = jnp.einsum(
        "td,thc->dhc", normed_one, grad_rates, preferred_element_type=jnp.float32
    )
    mixer_in_part = jnp.einsum(
        "thc,dhc->td", grad_mixed, w_mix, preferred_element_type=jnp.float32
    ) + jnp.einsum("thc,dhc->td", grad_rates, w_rate, preferred_element_type=jnp.float32)
    mixer_in = lax.psum(mixer_in_part.astype(jnp.bfloat16), "tp").astype(jnp.float32)
    gain_one_grad = jnp.sum(mixer_in_part * x_hat_one, axis=0)
    grad_tokens = (grad_residual + norm_back(mixer_in, gain_one, x_hat_one, scale_one)).astype(
        jnp.bfloat16
    )
    seq_index = lax.axis_index("seq")
    tp_count = lax.axis_size("tp")
    seq_parts = (gain_one_grad, gain_two_grad, out_gain_grad, conv_grad, a_log_grad, dt_bias_grad)
    seq_summed = own_then_peers(
        jnp.concatenate([part.reshape(-1) for part in seq_parts] + [grad_rate.reshape(-1)]),
        "seq",
        3,
    )
    seq_summed = jnp.sum(seq_summed, axis=0)
    tp_size = sum(part.size for part in seq_parts)
    rate_rows = grad_rate.shape[0] // lax.axis_size("seq")
    rate_sum = lax.dynamic_slice_in_dim(
        seq_summed[tp_size:].reshape(grad_rate.shape), seq_index * rate_rows, rate_rows, 0
    )
    by_tp = own_then_peers(seq_summed[:tp_size], "tp", 4)
    small_sums = []
    start_at = 0
    for part in seq_parts:
        piece = by_tp[:, start_at : start_at + part.size]
        start_at += part.size
        if part.ndim == 1 and part.shape[0] != head_count:
            small_sums.append(jnp.sum(piece, axis=0))
        elif part.ndim == 1:
            small_sums.append(piece.reshape(tp_count * head_count))
        else:
            small_sums.append(
                jnp.moveaxis(piece.reshape((tp_count,) + part.shape), 0, 1).reshape(
                    (taps_all, tp_count * head_count, conv_width)
                )
            )
    weight_sums = (
        lax.psum_scatter(
            grad_mix.astype(jnp.bfloat16), "seq", scatter_dimension=0, tiled=True
        ).astype(jnp.float32),
        rate_sum,
        early_sums[0].astype(jnp.float32),
        early_sums[1].astype(jnp.float32),
        early_sums[2].astype(jnp.float32),
    )
    return (
        layer_out,
        grad_tokens,
        small_sums[0],
        weight_sums[0],
        weight_sums[1],
        small_sums[3],
        small_sums[4],
        small_sums[5],
        small_sums[2],
        weight_sums[2],
        small_sums[1],
        weight_sums[3],
        weight_sums[4],
    )


def solution(mesh):
    in_specs = (
        P("seq", None),
        P("seq"),
        P(),
        P(None, "tp", None),
        P(None, "tp", None),
        P(None, "tp", None),
        P("tp"),
        P("tp"),
        P(),
        P(None, "tp", None),
        P(),
        P(None, None, "tp"),
        P(None, "tp"),
        P("seq", None),
    )
    out_specs = (
        P("seq", None),
        P("seq", None),
        P(),
        P("seq", "tp", None),
        P("seq", "tp", None),
        P(),
        P(),
        P(),
        P(),
        P("seq", "tp", None),
        P(),
        P("seq", None, "tp"),
        P("seq", "tp"),
    )
    return jax.shard_map(shards, mesh=mesh, in_specs=in_specs, out_specs=out_specs, check_vma=False)
```

```python
import functools

import jax
import jax.numpy as jnp
from jax import lax
from jax.experimental import pallas as pl
from jax.experimental.pallas import tpu as pltpu
from jax.sharding import PartitionSpec as P

MESH_IDS = pl.DeviceIdType.MESH

DK = 128
GROUP = 64


EPSILON = 1e-06
EXACT_ARITHMETIC = lax.Precision.HIGHEST
FAST_ARITHMETIC = lax.Precision.HIGH


def shifted(block, axis, distance):
    devices = range(lax.axis_size(axis))
    route = [(i - distance, i) for i in devices if i - distance in devices]
    return lax.ppermute(block, axis, route)


def peer_gather_kernel(axis, count, mode, x_ref, out_ref, send_sem, recv_sem):
    me = lax.axis_index(axis)
    barrier = pltpu.get_barrier_semaphore()
    for step in range(1, count):
        pl.semaphore_signal(
            barrier, inc=1, device_id={axis: lax.rem(me + step, count)}, device_id_type=MESH_IDS
        )
    pl.semaphore_wait(barrier, count - 1)

    def link(step, source, target):
        return pltpu.make_async_remote_copy(
            src_ref=x_ref,
            dst_ref=out_ref.at[source],
            send_sem=send_sem.at[step],
            recv_sem=recv_sem.at[step],
            device_id={axis: target},
            device_id_type=MESH_IDS,
        )

    def target_of(step):
        if mode == "up":
            return me + step, me + step < count
        if mode == "down":
            return me - step, me - step >= 0
        return lax.rem(me + step, count), me >= 0

    def source_of(step):
        if mode == "up":
            return me - step, me - step >= 0
        if mode == "down":
            return me + step, me + step < count
        return lax.rem(me + count - step, count), me >= 0

    for step in range(1, count):
        target, sending = target_of(step)

        @pl.when(sending)
        def _():
            link(step, me, target).start()

    for step in range(1, count):
        target, sending = target_of(step)
        source, receiving = source_of(step)

        @pl.when(sending)
        def _():
            link(step, me, target).wait_send()

        @pl.when(receiving)
        def _():
            link(step, source, source).wait_recv()


def peer_gather(x, axis, mode, collective_id):
    count = lax.axis_size(axis)
    return pl.pallas_call(
        functools.partial(peer_gather_kernel, axis, count, mode),
        out_shape=jax.ShapeDtypeStruct((count,) + x.shape, x.dtype),
        in_specs=[pl.BlockSpec(memory_space=pl.ANY)],
        out_specs=pl.BlockSpec(memory_space=pl.ANY),
        scratch_shapes=[pltpu.SemaphoreType.DMA((count,)), pltpu.SemaphoreType.DMA((count,))],
        compiler_params=pltpu.CompilerParams(collective_id=collective_id, has_side_effects=True),
    )(x)


def joined_gather(value, axis, mode, collective_id, kind):
    widths = [part.shape[-1] for part in value]
    packed = jnp.concatenate([part.astype(kind) for part in value], axis=-1)
    gathered = peer_gather(packed, axis, mode, collective_id)
    pieces = []
    start_at = 0
    for width in widths:
        pieces.append(gathered[..., start_at : start_at + width])
        start_at += width
    return tuple(pieces)


def carried_in(value, axis, join, neutral):
    place = lax.axis_index(axis)
    gathered = joined_gather(value, axis, "up", 1, jnp.bfloat16)
    state = jax.tree.map(lambda a, e: jnp.zeros_like(a) + jnp.asarray(e, a.dtype), value, neutral)

    def one(lap, state):
        return join(
            state,
            jax.tree.map(
                lambda a, own: lax.dynamic_index_in_dim(a, lap, 0, False).astype(own.dtype),
                gathered,
                value,
            ),
        )

    return lax.fori_loop(0, place, one, state)


def carried_in_2(value, axis, join, neutral):
    count, mine = (lax.axis_size(axis), lax.axis_index(axis))
    pieces = jax.tree.map(
        lambda part: lax.all_gather(part.astype(jnp.bfloat16), axis).astype(part.dtype), value
    )
    pieces = jax.tree.map(lambda part: part[::-1], pieces)
    mine = count - 1 - mine
    running = jax.tree.map(
        lambda part, zero: jnp.full_like(part, 0) + jnp.asarray(zero, part.dtype), value, neutral
    )

    def lap(position, running):
        longer = join(running, jax.tree.map(lambda part: part[position], pieces))
        return jax.tree.map(lambda new, old: jnp.where(position < mine, new, old), longer, running)

    return lax.fori_loop(0, count - 1, lap, running)


def own_then_peers(flat, axis, collective_id):
    size = flat.shape[0]
    padded = -(-size // 1024) * 1024
    tiles = jnp.pad(flat, (0, padded - size)).reshape(padded // 128, 128)
    gathered = peer_gather(tiles, axis, "all", collective_id)
    slots = lax.broadcasted_iota(jnp.int32, gathered.shape, 0)
    filled = jnp.where(slots == lax.axis_index(axis), tiles[None], gathered)
    return filled.reshape(gathered.shape[0], padded)[:, :size]


def rounded(values):
    return values.astype(jnp.bfloat16).astype(jnp.float32)


def norm_scale(values):
    return lax.rsqrt(jnp.mean(values * values, axis=-1, keepdims=True) + EPSILON)


def unit_rows(values):
    return values * lax.rsqrt(jnp.sum(values * values, axis=-1, keepdims=True) + EPSILON)


def norm_back(grad_normed, gain_f, x_hat, scales):
    shaped = grad_normed * gain_f
    return scales * (shaped - x_hat * jnp.mean(shaped * x_hat, axis=-1, keepdims=True))


def conv_features(padded, weights, keeping):
    taps_all = weights.shape[0]
    length = keeping.shape[1]
    summed = weights[taps_all - 1] * padded[taps_all - 1 :]
    for offset in range(1, taps_all):
        begin_at = taps_all - 1 - offset
        summed = (
            summed
            + weights[begin_at]
            * padded[begin_at : begin_at + length]
            * keeping[offset - 1][:, None, None]
        )
    active = jax.nn.silu(summed)
    return (unit_rows(active[..., :DK]), unit_rows(active[..., DK : 2 * DK]), active[..., 2 * DK :])


def rate_terms(rate_rows, a_log, dt_bias):
    strength = jax.nn.sigmoid(rate_rows[..., 1])
    log_decay = -jnp.exp(a_log) * jax.nn.softplus(rate_rows[..., 0] + dt_bias)
    return (strength, log_decay)


def gated_norm(core_rows, gate_rows, gain_rows):
    return core_rows * norm_scale(core_rows) * gain_rows * jax.nn.silu(gate_rows)


def swiglu(gate_up):
    return jax.nn.silu(gate_up[:, 0]) * gate_up[:, 1]


def batched_mm(left_mat, right_mat):
    return jnp.einsum("hij,hjk->hik", left_mat, right_mat, precision=FAST_ARITHMETIC)


def compose(earlier, later):
    return (batched_mm(later[0], earlier[0]), batched_mm(later[0], earlier[1]) + later[1])


def unit_lower_inverse(lower_mat):
    size = lower_mat.shape[-1]
    rows = lax.broadcasted_iota(jnp.int32, (size, size), 0)
    cols = lax.broadcasted_iota(jnp.int32, (size, size), 1)
    eye = (rows == cols).astype(lower_mat.dtype)
    strict = lower_mat - eye
    inverse = eye
    width = 1
    while width < size:
        within = ((rows // (2 * width)) == (cols // (2 * width))) & (
            (rows // width) != (cols // width)
        )
        off = strict * within.astype(lower_mat.dtype)
        if width == 1:
            inverse = eye - off
        else:
            inverse = inverse - jnp.einsum(
                "...ij,...jk->...ik",
                inverse,
                jnp.einsum("...ij,...jk->...ik", off, inverse, precision=FAST_ARITHMETIC),
                precision=FAST_ARITHMETIC,
            )
        width *= 2
    return inverse


def delta_local(query, keys, values, strength, log_decay, resets):
    length, head_count, key_size = keys.shape
    payload_dimension = values.shape[-1]
    number_of_segments = length // GROUP

    def blocked(array):
        shaped = array.reshape((number_of_segments, GROUP, head_count) + array.shape[2:])
        return jnp.moveaxis(shaped, 2, 1)

    stacked = jnp.concatenate(
        [values, jnp.zeros((length, head_count, key_size), jnp.float32)], axis=-1
    )
    query_b = blocked(query * key_size ** (-0.5))
    keys_b = blocked(keys)
    stacked_b = blocked(stacked)
    strength_b = blocked(strength)
    decay_sum = jnp.cumsum(blocked(log_decay), axis=-1)
    pieces = jnp.cumsum(resets.reshape(number_of_segments, GROUP), axis=-1)
    row_ids = lax.broadcasted_iota(jnp.int32, (GROUP, GROUP), 0)
    col_ids = lax.broadcasted_iota(jnp.int32, (GROUP, GROUP), 1)
    joined = pieces[:, :, None] == pieces[:, None, :]
    inside = (joined & (row_ids >= col_ids))[:, None].astype(jnp.float32)
    before = (joined & (row_ids > col_ids))[:, None].astype(jnp.float32)
    spread = decay_sum[..., :, None] - decay_sum[..., None, :]
    decays = jnp.exp(jnp.where(inside > 0, spread, 0.0)) * inside
    from_start = jnp.exp(decay_sum) * (pieces == 0)[:, None, :].astype(jnp.float32)
    to_end = jnp.exp(decay_sum[..., -1:] - decay_sum) * (pieces == pieces[:, -1:])[
        :, None, :
    ].astype(jnp.float32)
    key_dots = jnp.einsum(
        "nhtk,nhjk->nhtj", keys_b, keys_b, preferred_element_type=jnp.float32
    )
    lower_mat = (
        jnp.eye(GROUP, dtype=jnp.float32) + key_dots * decays * before * strength_b[..., :, None]
    )

    inverse = unit_lower_inverse(lower_mat)

    def solved(rhs_rows):
        return jnp.einsum("nhtj,nhjw->nhtw", inverse, rhs_rows, precision=FAST_ARITHMETIC)

    value_part = solved(strength_b[..., None] * stacked_b)
    state_part = solved((strength_b * from_start)[..., None] * keys_b)
    query_keys = (
        jnp.einsum("nhtk,nhjk->nhtj", blocked(query), keys_b, preferred_element_type=jnp.float32)
        * key_size ** (-0.5)
        * decays
    )
    end_keys = to_end[..., None] * keys_b
    initial = jnp.concatenate(
        [
            jnp.zeros((head_count, key_size, payload_dimension), jnp.float32),
            jnp.broadcast_to(
                jnp.eye(key_size, dtype=jnp.float32), (head_count, key_size, key_size)
            ),
        ],
        axis=-1,
    )

    def advance(carried_state, inputs):
        value_rows, state_rows, query_rows, mixing, end_rows, start_decay, block_decay = inputs
        new_values = value_rows - jnp.einsum(
            "htk,hkw->htw", state_rows, carried_state, precision=FAST_ARITHMETIC
        )
        emitted = start_decay[..., None] * jnp.einsum(
            "htk,hkw->htw", query_rows, carried_state, precision=FAST_ARITHMETIC
        ) + jnp.einsum("htj,hjw->htw", mixing, new_values, precision=FAST_ARITHMETIC)
        carried_state = block_decay[:, None, None] * carried_state + jnp.einsum(
            "hjk,hjw->hkw", end_rows, new_values, precision=FAST_ARITHMETIC
        )
        return (carried_state, emitted)

    final_state, emitted_all = lax.scan(
        advance,
        initial,
        (value_part, state_part, query_b, query_keys, end_keys, from_start, from_start[..., -1]),
        unroll=True,
    )
    emitted_all = jnp.moveaxis(emitted_all, 1, 2).reshape(
        length, head_count, payload_dimension + key_size
    )
    return (
        emitted_all[..., :payload_dimension],
        emitted_all[..., payload_dimension:],
        final_state[..., :payload_dimension],
        final_state[..., payload_dimension:],
    )


def shards(
    tokens,
    seg_ids,
    norm1_gain,
    w_mix,
    w_rate,
    conv_w,
    a_log,
    dt_bias,
    out_gain,
    w_out,
    norm2_gain,
    w_up,
    w_down,
    cotangent,
):
    length = tokens.shape[0]
    head_count = w_mix.shape[1]
    taps_all = conv_w.shape[0]
    rim_rows = taps_all - 1
    conv_width = conv_w.shape[2]
    tp_index = lax.axis_index("tp")
    tokens_f = tokens.astype(jnp.float32)
    gain_one = norm1_gain.astype(jnp.float32)
    scale_one = norm_scale(tokens_f)
    x_hat_one = tokens_f * scale_one
    normed_one = (x_hat_one * gain_one).astype(jnp.bfloat16)
    mixed = jnp.einsum("td,dhc->thc", normed_one, w_mix, preferred_element_type=jnp.float32)
    rate_rows = jnp.einsum("td,dhc->thc", normed_one, w_rate, preferred_element_type=jnp.float32)
    conv_rows = mixed[..., :conv_width].astype(jnp.bfloat16)
    gate_rows = mixed[..., conv_width:]
    tail_rows, tail_ids = shifted(
        (conv_rows[length - rim_rows :], seg_ids[length - rim_rows :].astype(jnp.bfloat16)),
        "seq",
        1,
    )
    own_ids = seg_ids.astype(jnp.float32)
    padded_ids = jnp.concatenate([tail_ids.astype(jnp.float32), own_ids])
    keeping = jnp.stack(
        [
            (padded_ids[rim_rows - offset : rim_rows - offset + length] == own_ids).astype(
                jnp.float32
            )
            for offset in range(1, taps_all)
        ]
    )
    resets = (padded_ids[rim_rows - 1 : rim_rows - 1 + length] != own_ids).astype(jnp.float32)
    padded = jnp.concatenate([tail_rows, conv_rows]).astype(jnp.float32)
    features, conv_pull = jax.vjp(
        lambda padded_rows, weights: conv_features(padded_rows, weights, keeping),
        padded,
        conv_w.astype(jnp.float32),
    )
    query = rounded(features[0])
    keys = rounded(features[1])
    values = rounded(features[2])
    (strength, log_decay), rate_pull = jax.vjp(rate_terms, rate_rows, a_log, dt_bias)
    (local_output, probe_destinations, base_state, transfer), delta_pull = jax.vjp(
        lambda q, k, v, b, g: delta_local(q, k, v, b, g, resets),
        query,
        keys,
        values,
        strength,
        log_decay,
    )
    zero_state = jnp.zeros_like(base_state)
    identity_mats = jnp.broadcast_to(jnp.eye(transfer.shape[1], dtype=jnp.float32), transfer.shape)
    entering_memory_matrix = carried_in(
        (transfer, base_state), "seq", compose, (identity_mats, zero_state)
    )[1]
    core_output = local_output + jnp.einsum(
        "vkq,kqp->vkp", probe_destinations, entering_memory_matrix, precision=FAST_ARITHMETIC
    )
    normed_out_f, gate_pull = jax.vjp(
        gated_norm, core_output, gate_rows, out_gain.astype(jnp.float32)
    )
    normed_out = normed_out_f.astype(jnp.bfloat16)
    mixer_part = jnp.einsum("thv,dhv->td", normed_out, w_out, preferred_element_type=jnp.float32)
    gain_two = norm2_gain.astype(jnp.float32)
    residual = tokens_f + lax.psum(mixer_part.astype(jnp.bfloat16), "tp").astype(jnp.float32)
    scale_two = norm_scale(residual)
    x_hat_two = residual * scale_two
    normed_two = (x_hat_two * gain_two).astype(jnp.bfloat16)
    gate_up = jnp.einsum("td,dcf->tcf", normed_two, w_up, preferred_element_type=jnp.float32)
    hidden_f, hidden_pull = jax.vjp(swiglu, gate_up)
    hidden = hidden_f.astype(jnp.bfloat16)
    ffn_part = jnp.einsum("tf,df->td", hidden, w_down, preferred_element_type=jnp.float32)
    grad_down = jnp.einsum("tf,td->df", hidden, cotangent, preferred_element_type=jnp.float32)
    grad_hidden = jnp.einsum("td,df->tf", cotangent, w_down, preferred_element_type=jnp.float32)
    grad_gate_up = hidden_pull(grad_hidden)[0].astype(jnp.bfloat16)
    grad_up = jnp.einsum(
        "td,tcf->dcf", normed_two, grad_gate_up, preferred_element_type=jnp.float32
    )
    ffn_in_part = jnp.einsum("tcf,dcf->td", grad_gate_up, w_up, preferred_element_type=jnp.float32)
    ffn_in = lax.psum(ffn_in_part.astype(jnp.bfloat16), "tp").astype(jnp.float32)
    gain_two_grad = jnp.sum(ffn_in_part * x_hat_two, axis=0)
    grad_residual = cotangent.astype(jnp.float32) + norm_back(
        ffn_in, gain_two, x_hat_two, scale_two
    )
    grad_mixer = grad_residual.astype(jnp.bfloat16)
    grad_w_out = jnp.einsum(
        "td,thv->dhv", grad_mixer, normed_out, preferred_element_type=jnp.float32
    )
    grad_normed_out = jnp.einsum(
        "td,dhv->thv", grad_mixer, w_out, preferred_element_type=jnp.float32
    )
    core_output_grad, grad_gate_rows, out_gain_grad = gate_pull(grad_normed_out)
    own_state_gradient = jnp.einsum(
        "eyc,eyn->ycn", probe_destinations, core_output_grad, precision=FAST_ARITHMETIC
    )
    transfer_t = jnp.swapaxes(transfer, 1, 2)
    state_gradient = carried_in_2(
        (transfer_t, own_state_gradient), "seq", compose, (identity_mats, zero_state)
    )[1]
    branch_derivatives = jnp.einsum(
        "xao,aeo->xae", core_output_grad, entering_memory_matrix, precision=FAST_ARITHMETIC
    )
    transfer_gradient = jnp.einsum(
        "zne,zye->zny", state_gradient, entering_memory_matrix, precision=FAST_ARITHMETIC
    )
    ffn_send, early_send, state_gradient = lax.optimization_barrier(
        (
            ffn_part.astype(jnp.bfloat16),
            tuple(part.astype(jnp.bfloat16) for part in (grad_w_out, grad_up, grad_down)),
            state_gradient,
        )
    )
    ffn_sum = lax.psum(ffn_send, "tp")
    early_sums = tuple(
        lax.psum_scatter(part, "seq", scatter_dimension=0, tiled=True) for part in early_send
    )
    delta_grads = delta_pull(
        (core_output_grad, branch_derivatives, state_gradient, transfer_gradient)
    )
    grad_query, grad_keys, grad_values, grad_strength, grad_decay = delta_grads
    grad_rate_rows, a_log_grad, dt_bias_grad = rate_pull((grad_strength, grad_decay))
    grad_padded, conv_grad = conv_pull((grad_query, grad_keys, grad_values))
    back_rows = shifted(grad_padded[:rim_rows], "seq", -1)
    grad_conv_rows = grad_padded[rim_rows:] + jnp.concatenate(
        [jnp.zeros((length - rim_rows,) + back_rows.shape[1:], jnp.float32), back_rows]
    )
    grad_mixed = jnp.concatenate([grad_conv_rows, grad_gate_rows], axis=-1).astype(jnp.bfloat16)
    ffn_sum, early_sums, grad_mixed = lax.optimization_barrier((ffn_sum, early_sums, grad_mixed))
    layer_out = (residual + ffn_sum.astype(jnp.float32)).astype(jnp.bfloat16)
    grad_rates = grad_rate_rows.astype(jnp.bfloat16)
    grad_mix = jnp.einsum("td,thc->dhc", normed_one, grad_mixed, preferred_element_type=jnp.float32)
    grad_rate = jnp.einsum(
        "td,thc->dhc", normed_one, grad_rates, preferred_element_type=jnp.float32
    )
    mixer_in_part = jnp.einsum(
        "thc,dhc->td", grad_mixed, w_mix, preferred_element_type=jnp.float32
    ) + jnp.einsum("thc,dhc->td", grad_rates, w_rate, preferred_element_type=jnp.float32)
    mixer_in = lax.psum(mixer_in_part.astype(jnp.bfloat16), "tp").astype(jnp.float32)
    gain_one_grad = jnp.sum(mixer_in_part * x_hat_one, axis=0)
    grad_tokens = (grad_residual + norm_back(mixer_in, gain_one, x_hat_one, scale_one)).astype(
        jnp.bfloat16
    )
    seq_index = lax.axis_index("seq")
    tp_count = lax.axis_size("tp")
    seq_parts = (gain_one_grad, gain_two_grad, out_gain_grad, conv_grad, a_log_grad, dt_bias_grad)
    seq_summed = own_then_peers(
        jnp.concatenate([part.reshape(-1) for part in seq_parts] + [grad_rate.reshape(-1)]),
        "seq",
        3,
    )
    seq_summed = jnp.sum(seq_summed, axis=0)
    tp_size = sum(part.size for part in seq_parts)
    rate_rows = grad_rate.shape[0] // lax.axis_size("seq")
    rate_sum = lax.dynamic_slice_in_dim(
        seq_summed[tp_size:].reshape(grad_rate.shape), seq_index * rate_rows, rate_rows, 0
    )
    by_tp = own_then_peers(seq_summed[:tp_size], "tp", 4)
    small_sums = []
    start_at = 0
    for part in seq_parts:
        piece = by_tp[:, start_at : start_at + part.size]
        start_at += part.size
        if part.ndim == 1 and part.shape[0] != head_count:
            small_sums.append(jnp.sum(piece, axis=0))
        elif part.ndim == 1:
            small_sums.append(piece.reshape(tp_count * head_count))
        else:
            small_sums.append(
                jnp.moveaxis(piece.reshape((tp_count,) + part.shape), 0, 1).reshape(
                    (taps_all, tp_count * head_count, conv_width)
                )
            )
    weight_sums = (
        lax.psum_scatter(
            grad_mix.astype(jnp.bfloat16), "seq", scatter_dimension=0, tiled=True
        ).astype(jnp.float32),
        rate_sum,
        early_sums[0].astype(jnp.float32),
        early_sums[1].astype(jnp.float32),
        early_sums[2].astype(jnp.float32),
    )
    return (
        layer_out,
        grad_tokens,
        small_sums[0],
        weight_sums[0],
        weight_sums[1],
        small_sums[3],
        small_sums[4],
        small_sums[5],
        small_sums[2],
        weight_sums[2],
        small_sums[1],
        weight_sums[3],
        weight_sums[4],
    )


def solution(mesh):
    in_specs = (
        P("seq", None),
        P("seq"),
        P(),
        P(None, "tp", None),
        P(None, "tp", None),
        P(None, "tp", None),
        P("tp"),
        P("tp"),
        P(),
        P(None, "tp", None),
        P(),
        P(None, None, "tp"),
        P(None, "tp"),
        P("seq", None),
    )
    out_specs = (
        P("seq", None),
        P("seq", None),
        P(),
        P("seq", "tp", None),
        P("seq", "tp", None),
        P(),
        P(),
        P(),
        P(),
        P("seq", "tp", None),
        P(),
        P("seq", None, "tp"),
        P("seq", "tp"),
    )
    return jax.shard_map(shards, mesh=mesh, in_specs=in_specs, out_specs=out_specs, check_vma=False)
```
